768 devices in a mesh: freq: 16 (over y_lo, x), rtile: 24 (over z, core), rep: 2 (over y_hi).
Axes of the slice: x: 4, y: 8 (y_hi: 2, y_lo: 4; y = y_hi * 4 + y_lo), z: 12, core: 2. Of those that a mesh axis runs over, the one named last changes fastest.
Arguments:
- model: bfloat16 [24, 512, 32, 1024], P('rtile', 'freq'), may hold values from -0.1796875 to 0.1796875
- green_left: bfloat16 [2, 48, 8, 48, 48, 256], P(None, 'freq', 'rep', 'rtile'), may hold values from -0.09375 to 0.09375
- green_right: bfloat16 [2, 48, 8, 48, 48, 256], P(None, 'freq', 'rep', 'rtile'), may hold values from -0.25 to 0.25
- ranks: int32 [48, 8, 48], P('freq', 'rep', 'rtile'), may hold values from 8 to 48
- data: float32 [2, 1536, 2048], P(None, ('freq', 'rtile'), 'rep'), may hold values from -3 to 3
Outputs:
- residual: float32 [2, 1536, 2048], P(None, ('freq', 'rtile'), 'rep')
- gradient: bfloat16 [24, 512, 32, 1024], P('rtile', ('freq', 'rep'))
The draws below stay inside these ranges and needn't reach their ends.
All inputs are finite; a program needn't handle non-finite values.
Results may differ from the reference program's by a relative error of at most 0.014.
Values may be sent and summed in bfloat16 or wider, within the bound.
A program may use at most 32 MiB of HBM per device.

```python
import math
import jax
import jax.numpy as jnp
from jax import lax

TILE = 256
RANK = 48
NS = 2048
NT = 1024
RHS = 32
CW = 512
NCT = 48
NR = 12288
ROWT = 8
NF = 48
N_RTILE = 24


def plant(drawn, rng, smallest, largest):
    place = [jax.random.randint(jax.random.fold_in(rng, axis), (), 0, length) for axis, length in enumerate(drawn.shape)]
    longest = drawn.shape.index(max(drawn.shape))
    beside = place[:longest] + [(place[longest] + 1) % drawn.shape[longest]] + place[longest + 1:]
    return drawn.at[tuple(place)].set(smallest).at[tuple(beside)].set(largest)


def block_levels(key, shape, shards, least, high):
    def one(dim, parts):
        draws = jax.random.uniform(jax.random.fold_in(jax.random.fold_in(key, 6), dim), (parts,), jnp.float32, least / len(shards), high / len(shards))
        return jnp.repeat(jnp.exp(draws), shape[dim] // parts).reshape((-1,) + (1,) * (len(shape) - dim - 1))

    level = one(*shards[0])
    for cut in shards[1:]:
        level = level * one(*cut)
    return level


def centred(key, dims, deviation, most, split=(), kind=jnp.bfloat16):
    loudness = block_levels(key, dims, split, -0.22, 0.18) if split else 1.0
    drawn = jax.random.normal(key, dims, jnp.float32) * deviation * loudness
    return jnp.minimum(jnp.maximum(drawn, -most), most).astype(kind)


def setup_inputs(seed: int = 0) -> dict:
    key_list = jax.random.split(jax.random.key(seed), 6)
    return {
        "model": centred(key_list[0], (N_RTILE, CW, RHS, NT), 0.03, 0.1796875, ((0, 24), (1, 16))),
        "green_left": centred(key_list[1], (2, NF, ROWT, NCT, RANK, TILE), (2 * RANK * NCT) ** -0.5, 0.09375, ((1, 16), (2, 2), (3, 24))),
        "green_right": centred(key_list[2], (2, NF, ROWT, NCT, RANK, TILE), (2 * TILE) ** -0.5, 0.25, ((1, 16), (2, 2), (3, 24))),
        "ranks": plant(jax.random.randint(key_list[3], (NF, ROWT, NCT), RANK // 6, RANK + 1), jax.random.fold_in(key_list[3], 1), RANK // 6, RANK).astype(jnp.int32),
        "data": centred(key_list[4], (2, NF * RHS, NS), 0.5, 3.0, ((1, 384), (2, 2)), jnp.float32),
    }


def tables(count, length):
    freq_bins = 1 + jnp.arange(count, dtype=jnp.int32)
    samples = jnp.arange(length, dtype=jnp.int32)
    phases = ((samples[:, None] * freq_bins[None, :]) % length).astype(jnp.float32) * (2.0 * math.pi / length)
    return jnp.cos(phases).astype(jnp.bfloat16), (-jnp.sin(phases)).astype(jnp.bfloat16)


def per_freq(inputs):
    left, right, spec, rank_row, observed = inputs
    left_re = left[0].astype(jnp.float32)
    left_im = left[1].astype(jnp.float32)
    right_re = right[0].astype(jnp.float32)
    right_im = right[1].astype(jnp.float32)
    spec_re = spec[0].astype(jnp.float32)
    spec_im = spec[1].astype(jnp.float32)
    rank_mask = (jnp.arange(RANK, dtype=jnp.int32)[None, None, :] < rank_row[:, :, None]).astype(jnp.float32)[..., None]
    proj_re = jnp.einsum("ijkn,jnr->ijkr", right_re, spec_re) + jnp.einsum("ijkn,jnr->ijkr", right_im, spec_im)
    proj_im = jnp.einsum("ijkn,jnr->ijkr", right_re, spec_im) - jnp.einsum("ijkn,jnr->ijkr", right_im, spec_re)
    proj_re = (proj_re * rank_mask).astype(jnp.bfloat16).astype(jnp.float32)
    proj_im = (proj_im * rank_mask).astype(jnp.bfloat16).astype(jnp.float32)
    out_re = jnp.einsum("ijks,ijkr->ris", left_re, proj_re) - jnp.einsum("ijks,ijkr->ris", left_im, proj_im)
    out_im = jnp.einsum("ijks,ijkr->ris", left_re, proj_im) + jnp.einsum("ijks,ijkr->ris", left_im, proj_re)
    predicted = jnp.stack([out_re, out_im]).reshape(2, RHS, NS)
    residual = predicted - observed
    misfit_low = residual.astype(jnp.bfloat16).astype(jnp.float32).reshape(2, RHS, ROWT, TILE)
    back_re = jnp.einsum("ijks,ris->ijkr", left_re, misfit_low[0]) + jnp.einsum("ijks,ris->ijkr", left_im, misfit_low[1])
    back_im = jnp.einsum("ijks,ris->ijkr", left_re, misfit_low[1]) - jnp.einsum("ijks,ris->ijkr", left_im, misfit_low[0])
    back_re = (back_re * rank_mask).astype(jnp.bfloat16).astype(jnp.float32)
    back_im = (back_im * rank_mask).astype(jnp.bfloat16).astype(jnp.float32)
    grad_re = jnp.einsum("ijkn,ijkr->jnr", right_re, back_re) - jnp.einsum("ijkn,ijkr->jnr", right_im, back_im)
    grad_im = jnp.einsum("ijkn,ijkr->jnr", right_re, back_im) + jnp.einsum("ijkn,ijkr->jnr", right_im, back_re)
    return residual, jnp.stack([grad_re, grad_im]).astype(jnp.bfloat16)


def reference(model, green_left, green_right, ranks, data):
    cosine, sine_neg = tables(NF, NT)
    traces = model.reshape(NR, RHS, NT).astype(jnp.float32)
    spec_re = jnp.einsum("mrt,tq->qmr", traces, cosine.astype(jnp.float32))
    spec_im = jnp.einsum("mrt,tq->qmr", traces, sine_neg.astype(jnp.float32))
    spectrum = jnp.stack([spec_re, spec_im], axis=1).astype(jnp.bfloat16).reshape(NF, 2, NCT, TILE, RHS)
    left_freq = jnp.moveaxis(green_left, 1, 0)
    right_freq = jnp.moveaxis(green_right, 1, 0)
    data_freq = jnp.moveaxis(data.reshape(2, NF, RHS, NS), 1, 0)
    residual, grad_spec = lax.map(per_freq, (left_freq, right_freq, spectrum, ranks, data_freq))
    residual = jnp.moveaxis(residual, 1, 0).reshape(2, NF * RHS, NS)
    grad_spec = grad_spec.reshape(NF, 2, NR, RHS).astype(jnp.float32)
    gradient = jnp.einsum("qmr,tq->mrt", grad_spec[:, 0], cosine.astype(jnp.float32))
    gradient = gradient + jnp.einsum("qmr,tq->mrt", grad_spec[:, 1], sine_neg.astype(jnp.float32))
    gradient = gradient.astype(jnp.bfloat16).reshape(N_RTILE, CW, RHS, NT)
    return residual, gradient
```

```python
import functools

import jax
import jax.numpy as jnp
import ml_dtypes
import numpy as np
from jax import lax
from jax.experimental import pallas as pl
from jax.experimental.pallas import tpu as pltpu
from jax.sharding import PartitionSpec as P

MESH = pl.DeviceIdType.MESH
BF16 = jnp.bfloat16
F32 = jnp.float32
LAST = (((1,), (1,)), ((), ()))
PLAIN = (((1,), (0,)), ((), ()))


def tables(count, length):
    bins = 1 + np.arange(count, dtype=np.int64)
    phases = (bins[:, None] * np.arange(length, dtype=np.int64)[None, :] % length).astype(
        np.float32
    ) * np.float32(2.0 * np.pi / length)
    both = np.concatenate([np.cos(phases), -np.sin(phases)], axis=0)
    return both.astype(ml_dtypes.bfloat16)


def matmul(form, first, second):
    return lax.dot_general(first, second, form, preferred_element_type=F32)


def lanes(shape):
    return lax.broadcasted_iota(jnp.int32, shape, len(shape) - 1)


def rows(shape):
    return lax.broadcasted_iota(jnp.int32, shape, len(shape) - 2)


def chain_kernel(
    dims,
    model_ref,
    left_ref,
    right_ref,
    ranks_ref,
    data_ref,
    table_ref,
    residual_ref,
    spec_ref,
    traces,
    table,
    left,
    right,
    stage,
    send_a,
    recv_a,
    weights,
    send_r,
    recv_sib,
    send_z,
    recv_z,
    recv_d,
    back,
    grads,
    send_g,
    recv_g,
    load_sem,
    out_sem,
    a_sem,
    sib_sem,
    z_sem,
    d_sem,
    swap_sem,
    g_sem,
):
    n_freq, n_rtile, n_rep = dims
    n_z = n_rtile // 2
    n_slot = n_freq * n_rep
    me_f = lax.axis_index("freq")
    me_t = lax.axis_index("rtile")
    me_p = lax.axis_index("rep")
    me_slot = me_f * n_rep + me_p
    me_z = me_t // 2
    me_c = me_t % 2
    sibling = {"rtile": me_z * 2 + (1 - me_c)}
    group = model_ref.shape[1] // n_rep
    freq_local, row_tiles, col_tiles, rank_size, tile_size = right.shape[1:]

    def slot_device(slot):
        return {"freq": slot // n_rep, "rep": slot % n_rep}

    def z_device(z):
        return {"rtile": z * 2 + me_c}

    def slots_like(send_sem, recv_sem):
        most = recv_a.at[pl.ds(0, n_slot - 1)]
        return pltpu.make_async_remote_copy(
            src_ref=most,
            dst_ref=most,
            send_sem=send_sem,
            recv_sem=recv_sem,
            device_id=sibling,
            device_id_type=MESH,
        )

    def zs_like(send_sem, recv_sem):
        most = recv_z.at[pl.ds(0, n_z - 1)]
        return pltpu.make_async_remote_copy(
            src_ref=most,
            dst_ref=most,
            send_sem=send_sem,
            recv_sem=recv_sem,
            device_id=sibling,
            device_id_type=MESH,
        )

    model_load = pltpu.make_async_copy(
        model_ref.at[0, pl.ds(me_p * group, group)], traces, load_sem.at[0]
    )
    table_load = pltpu.make_async_copy(table_ref, table, load_sem.at[1])
    right_load = pltpu.make_async_copy(right_ref, right, load_sem.at[2])
    left_load = pltpu.make_async_copy(left_ref, left, load_sem.at[3])
    model_load.start()
    table_load.start()
    right_load.start()
    left_load.start()

    barrier = pltpu.get_barrier_semaphore()

    @pl.loop(1, n_slot)
    def _(step):
        pl.semaphore_signal(
            barrier, inc=1, device_id=slot_device((me_slot + step) % n_slot), device_id_type=MESH
        )

    @pl.loop(1, n_z)
    def _(step):
        pl.semaphore_signal(
            barrier, inc=1, device_id=z_device((me_z + step) % n_z), device_id_type=MESH
        )

    pl.semaphore_signal(barrier, inc=1, device_id=sibling, device_id_type=MESH)

    table_load.wait()
    model_load.wait()
    bins = n_freq * freq_local
    traces_2d = traces[...].reshape(group * traces.shape[1], traces.shape[2])
    spectra = matmul(LAST, table[...], traces_2d)
    quarter = lanes((bins, 128)) // 32
    for chunk in range(group // 4):
        re = spectra[:bins, chunk * 128 : (chunk + 1) * 128]
        im = spectra[bins:, chunk * 128 : (chunk + 1) * 128]
        first = jnp.where(
            quarter == 0,
            re,
            jnp.where(
                quarter == 1,
                pltpu.roll(im, 32, 1),
                jnp.where(quarter == 2, pltpu.roll(re, 32, 1), pltpu.roll(im, 64, 1)),
            ),
        )
        second = jnp.where(
            quarter == 0,
            pltpu.roll(re, 64, 1),
            jnp.where(
                quarter == 1,
                pltpu.roll(im, 96, 1),
                jnp.where(quarter == 2, pltpu.roll(re, 96, 1), im),
            ),
        )
        stage[pl.ds(2 * chunk, bins, stride=8), :] = first
        stage[pl.ds(2 * chunk + 1, bins, stride=8), :] = second
    band = freq_local * 8
    send_a[...] = stage[...].reshape(n_freq, band, 128).astype(BF16)

    pl.semaphore_wait(barrier, n_slot - 1 + n_z)

    def a_copy(target, source):
        return pltpu.make_async_remote_copy(
            src_ref=send_a.at[target // n_rep],
            dst_ref=recv_a.at[source],
            send_sem=out_sem.at[0],
            recv_sem=a_sem,
            device_id=slot_device(target),
            device_id_type=MESH,
        )

    @pl.loop(1, n_slot)
    def _(step):
        a_copy((me_slot + step) % n_slot, me_slot).start()

    recv_a[me_slot] = send_a[me_f]
    right_load.wait()
    left_load.wait()

    slots_like(out_sem.at[0], a_sem).wait_recv()

    per_tile = n_slot // col_tiles
    lane_p = lanes((row_tiles * rank_size, 128))
    row_k = rows((rank_size, 128))
    for f in range(freq_local):
        for j in range(col_tiles):
            arrived = recv_a[j * per_tile : (j + 1) * per_tile, f * 8 : (f + 1) * 8, :]
            arrived = arrived.astype(F32).reshape(per_tile * 8, 128)
            weights[pl.ds(0, per_tile * 8, stride=2), :] = arrived
            weights[pl.ds(1, per_tile * 8, stride=2), :] = pltpu.roll(arrived, 64, 1)
            columns = weights[...].astype(BF16)
            by_re = matmul(
                PLAIN, right[0, f, :, j].reshape(row_tiles * rank_size, tile_size), columns
            )
            by_im = matmul(
                PLAIN, right[1, f, :, j].reshape(row_tiles * rank_size, tile_size), columns
            )
            projected = by_re + jnp.where(
                lane_p < 32, pltpu.roll(by_im, 96, 1), -pltpu.roll(by_im, 32, 1)
            )
            for i in range(row_tiles):
                part = projected[i * rank_size : (i + 1) * rank_size]
                back[f, i, j * rank_size : (j + 1) * rank_size, :] = jnp.where(
                    row_k < ranks_ref[f, i, j], part, 0.0
                )
    low4 = rows((32, tile_size)) % 8 < 4
    for f in range(freq_local):
        for i in range(row_tiles):
            lhs = back[f, i].T[:64].astype(BF16)
            span = slice(i * tile_size, (i + 1) * tile_size)
            by_re = matmul(PLAIN, lhs, left[0, f, i].reshape(col_tiles * rank_size, tile_size))
            by_im = matmul(PLAIN, lhs, left[1, f, i].reshape(col_tiles * rank_size, tile_size))
            out_re = by_re[:32] - by_im[32:]
            out_im = by_re[32:] + by_im[:32]
            even = jnp.where(low4, out_re, pltpu.roll(out_im, 4, 0))
            odd = jnp.where(low4, pltpu.roll(out_re, 28, 0), out_im)
            send_r[0, f * 4 : (f + 1) * 4, :, span] = even.reshape(4, 8, tile_size).astype(BF16)
            send_r[1, f * 4 : (f + 1) * 4, :, span] = odd.reshape(4, 8, tile_size).astype(BF16)

    sib_copy = pltpu.make_async_remote_copy(
        src_ref=send_r.at[1 - me_c],
        dst_ref=recv_sib,
        send_sem=out_sem.at[1],
        recv_sem=sib_sem,
        device_id=sibling,
        device_id_type=MESH,
    )
    sib_copy.start()
    sib_copy.wait_recv()
    send_z[...] = (send_r[me_c].astype(F32) + recv_sib[...].astype(F32)).astype(BF16)

    def z_copy(target, source):
        return pltpu.make_async_remote_copy(
            src_ref=send_z.at[target],
            dst_ref=recv_z.at[source],
            send_sem=out_sem.at[2],
            recv_sem=z_sem,
            device_id=z_device(target),
            device_id_type=MESH,
        )

    @pl.loop(1, n_z)
    def _(step):
        z_copy((me_z + step) % n_z, me_z).start()

    recv_z[me_z] = send_z[me_z]

    zs_like(out_sem.at[2], z_sem).wait_recv()

    total = recv_z[0].astype(F32)
    for z in range(1, n_z):
        total = total + recv_z[z].astype(F32)
    residual_re = total[:4] - data_ref[0]
    residual_im = total[4:] - data_ref[1]
    residual_ref[0] = residual_re
    residual_ref[1] = residual_im
    recv_d[me_c, me_z] = jnp.concatenate([residual_re, residual_im], axis=0).astype(BF16)

    def d_copy(target, source):
        return pltpu.make_async_remote_copy(
            src_ref=recv_d.at[me_c, source],
            dst_ref=recv_d.at[me_c, source],
            send_sem=out_sem.at[3],
            recv_sem=d_sem,
            device_id=z_device(target),
            device_id_type=MESH,
        )

    @pl.loop(1, n_z)
    def _(step):
        d_copy((me_z + step) % n_z, me_z).start()

    zs_like(out_sem.at[3], d_sem).wait_recv()

    swap = pltpu.make_async_remote_copy(
        src_ref=recv_d.at[me_c],
        dst_ref=recv_d.at[me_c],
        send_sem=out_sem.at[4],
        recv_sem=swap_sem,
        device_id=sibling,
        device_id_type=MESH,
    )
    swap.start()
    swap.wait_recv()

    low4 = rows((32, recv_d.shape[3])) % 8 < 4
    row_k = rows((rank_size, 128))
    for f in range(freq_local):
        even = recv_d[0, f * 4 : (f + 1) * 4].astype(F32).reshape(32, -1)
        odd = recv_d[1, f * 4 : (f + 1) * 4].astype(F32).reshape(32, -1)
        mis_re = jnp.where(low4, even, pltpu.roll(odd, 4, 0))
        mis_im = jnp.where(low4, pltpu.roll(even, 28, 0), odd)
        top = jnp.concatenate([mis_re, mis_im, -mis_im, mis_re], axis=0).astype(BF16)
        low = jnp.concatenate([mis_im, -mis_re, mis_re, mis_im], axis=0).astype(BF16)
        for i in range(row_tiles):
            span = slice(i * tile_size, (i + 1) * tile_size)
            part = matmul(
                LAST, left[0, f, i].reshape(col_tiles * rank_size, tile_size), top[:, span]
            ) + matmul(
                LAST, left[1, f, i].reshape(col_tiles * rank_size, tile_size), low[:, span]
            )
            for j in range(col_tiles):
                grads[j, i * rank_size : (i + 1) * rank_size, :] = jnp.where(
                    row_k < ranks_ref[f, i, j], part[j * rank_size : (j + 1) * rank_size], 0.0
                )
        for j in range(col_tiles):
            lhs = grads[j].T.astype(BF16)
            spec_t = matmul(
                PLAIN, lhs[:64], right[0, f, :, j].reshape(row_tiles * rank_size, tile_size)
            ) + matmul(
                PLAIN, lhs[64:], right[1, f, :, j].reshape(row_tiles * rank_size, tile_size)
            )
            weights[:, :64] = spec_t.T
            even = weights[pl.ds(0, per_tile * 8, stride=2), :]
            odd = weights[pl.ds(1, per_tile * 8, stride=2), :]
            packed = jnp.where(lanes(even.shape) < 64, even, pltpu.roll(odd, 64, 1))
            send_g[j * per_tile : (j + 1) * per_tile, f * 8 : (f + 1) * 8, :] = packed.reshape(
                per_tile, 8, 128
            ).astype(BF16)

    def g_copy(target, source):
        return pltpu.make_async_remote_copy(
            src_ref=send_g.at[target],
            dst_ref=recv_g.at[source],
            send_sem=out_sem.at[5],
            recv_sem=g_sem,
            device_id=slot_device(target),
            device_id_type=MESH,
        )

    @pl.loop(1, n_slot)
    def _(step):
        g_copy((me_slot + step) % n_slot, me_slot).start()

    recv_g[me_slot] = send_g[me_slot]

    slots_like(out_sem.at[5], g_sem).wait_recv()

    for f in range(n_freq):
        both = recv_g[n_rep * f].astype(F32)
        for p in range(1, n_rep):
            both = both + recv_g[n_rep * f + p].astype(F32)
        stage[f * band : (f + 1) * band, :] = both
    for chunk in range(group // 4):
        first = stage[pl.ds(2 * chunk, bins, stride=8), :]
        second = stage[pl.ds(2 * chunk + 1, bins, stride=8), :]
        re = jnp.where(
            quarter == 0,
            first,
            jnp.where(
                quarter == 1,
                pltpu.roll(first, 96, 1),
                jnp.where(quarter == 2, pltpu.roll(second, 64, 1), pltpu.roll(second, 32, 1)),
            ),
        )
        im = jnp.where(
            quarter == 0,
            pltpu.roll(first, 96, 1),
            jnp.where(
                quarter == 1,
                pltpu.roll(first, 64, 1),
                jnp.where(quarter == 2, pltpu.roll(second, 32, 1), second),
            ),
        )
        spec_ref[:bins, chunk * 128 : (chunk + 1) * 128] = re.astype(BF16)
        spec_ref[bins:, chunk * 128 : (chunk + 1) * 128] = im.astype(BF16)

    slots_like(out_sem.at[0], a_sem).wait_send()
    zs_like(out_sem.at[2], z_sem).wait_send()
    zs_like(out_sem.at[3], d_sem).wait_send()
    slots_like(out_sem.at[5], g_sem).wait_send()
    sib_copy.wait_send()
    swap.wait_send()


def traces_kernel(spec_ref, table_ref, raw_ref, residual_ref, gradient_ref):
    residual_ref[...] = raw_ref[...]
    lhs = spec_ref[...].astype(F32).T.astype(BF16)
    out = matmul(PLAIN, lhs, table_ref[...])
    gradient_ref[...] = out.reshape(gradient_ref.shape).astype(BF16)


def shards(dims, model, green_left, green_right, ranks, data):
    n_freq, n_rtile, n_rep = dims
    n_z = n_rtile // 2
    n_slot = n_freq * n_rep
    _, receivers, rhs_count, length = model.shape
    group = receivers // n_rep
    freq_local = ranks.shape[0]
    row_tiles, col_tiles, rank_size, tile_size = green_left.shape[2:]
    bins = n_freq * freq_local
    sources = row_tiles * tile_size
    assert (rhs_count, tile_size, group, col_tiles) == (32, 256, 16, 2)
    assert n_z == freq_local * 4 and n_slot * group == col_tiles * tile_size
    table = jnp.asarray(tables(bins, length))
    band = freq_local * 8
    raw, spec = pl.pallas_call(
        functools.partial(chain_kernel, dims),
        out_shape=(
            jax.ShapeDtypeStruct(data.shape, F32),
            jax.ShapeDtypeStruct((2 * bins, group * rhs_count), BF16),
        ),
        in_specs=[
            pl.BlockSpec(memory_space=pl.ANY),
            pl.BlockSpec(memory_space=pl.ANY),
            pl.BlockSpec(memory_space=pl.ANY),
            pl.BlockSpec(memory_space=pltpu.SMEM),
            pl.BlockSpec(memory_space=pltpu.VMEM),
            pl.BlockSpec(memory_space=pl.ANY),
        ],
        out_specs=(
            pl.BlockSpec(memory_space=pltpu.VMEM),
            pl.BlockSpec(memory_space=pltpu.VMEM),
        ),
        scratch_shapes=[
            pltpu.VMEM((group, rhs_count, length), BF16),
            pltpu.VMEM((2 * bins, length), BF16),
            pltpu.VMEM(green_left.shape, BF16),
            pltpu.VMEM(green_right.shape, BF16),
            pltpu.VMEM((bins * 8, 128), F32),
            pltpu.VMEM((n_freq, band, 128), BF16),
            pltpu.VMEM((n_slot, band, 128), BF16),
            pltpu.VMEM((tile_size, 128), F32),
            pltpu.VMEM((2, n_z, 8, sources), BF16),
            pltpu.VMEM((n_z, 8, sources), BF16),
            pltpu.VMEM((n_z, 8, sources), BF16),
            pltpu.VMEM((n_z, 8, sources), BF16),
            pltpu.VMEM((2, n_z, 8, sources), BF16),
            pltpu.VMEM((freq_local, row_tiles, col_tiles * rank_size, 128), F32),
            pltpu.VMEM((col_tiles, row_tiles * rank_size, 128), F32),
            pltpu.VMEM((n_slot, band, 128), BF16),
            pltpu.VMEM((n_slot, band, 128), BF16),
            pltpu.SemaphoreType.DMA((4,)),
            pltpu.SemaphoreType.DMA((6,)),
            pltpu.SemaphoreType.DMA,
            pltpu.SemaphoreType.DMA,
            pltpu.SemaphoreType.DMA,
            pltpu.SemaphoreType.DMA,
            pltpu.SemaphoreType.DMA,
            pltpu.SemaphoreType.DMA,
        ],
        compiler_params=pltpu.CompilerParams(
            collective_id=0, has_side_effects=True, vmem_limit_bytes=48 * 1024 * 1024
        ),
    )(model, green_left, green_right, ranks, data, table)
    steps = 4
    residual, gradient = pl.pallas_call(
        traces_kernel,
        grid=(steps,),
        out_shape=(
            jax.ShapeDtypeStruct(data.shape, F32),
            jax.ShapeDtypeStruct((1, group, rhs_count, length), BF16),
        ),
        in_specs=[
            pl.BlockSpec((2 * bins, group * rhs_count // steps), lambda step: (0, step)),
            pl.BlockSpec((2 * bins, length), lambda step: (0, 0)),
            pl.BlockSpec(data.shape, lambda step: (0, 0, 0)),
        ],
        out_specs=(
            pl.BlockSpec(data.shape, lambda step: (0, 0, 0)),
            pl.BlockSpec((1, group // steps, rhs_count, length), lambda step: (0, step, 0, 0)),
        ),
    )(spec, table, raw)
    return (residual, gradient)


def solution(mesh):
    dims = tuple(mesh.shape[name] for name in ("freq", "rtile", "rep"))
    return jax.shard_map(
        functools.partial(shards, dims),
        mesh=mesh,
        in_specs=(
            P("rtile", "freq", None, None),
            P(None, "freq", "rep", "rtile", None, None),
            P(None, "freq", "rep", "rtile", None, None),
            P("freq", "rep", "rtile"),
            P(None, ("freq", "rtile"), "rep"),
        ),
        out_specs=(P(None, ("freq", "rtile"), "rep"), P("rtile", ("freq", "rep"), None, None)),
        check_vma=False,
    )
```

```python
import functools

import jax
import jax.numpy as jnp
import ml_dtypes
import numpy as np
from jax import lax
from jax.experimental import pallas as pl
from jax.experimental.pallas import tpu as pltpu
from jax.sharding import PartitionSpec as P

MESH = pl.DeviceIdType.MESH
BF16 = jnp.bfloat16
F32 = jnp.float32
LAST = (((1,), (1,)), ((), ()))
PLAIN = (((1,), (0,)), ((), ()))


def tables(count, length):
    bins = 1 + np.arange(count, dtype=np.int64)
    phases = (bins[:, None] * np.arange(length, dtype=np.int64)[None, :] % length).astype(
        np.float32
    ) * np.float32(2.0 * np.pi / length)
    both = np.concatenate([np.cos(phases), -np.sin(phases)], axis=0)
    return both.astype(ml_dtypes.bfloat16)


def matmul(form, first, second):
    return lax.dot_general(first, second, form, preferred_element_type=F32)


def lanes(shape):
    return lax.broadcasted_iota(jnp.int32, shape, len(shape) - 1)


def rows(shape):
    return lax.broadcasted_iota(jnp.int32, shape, len(shape) - 2)


def chain_kernel(
    dims,
    model_ref,
    left_ref,
    right_ref,
    ranks_ref,
    data_ref,
    table_ref,
    residual_ref,
    spec_ref,
    traces,
    table,
    left,
    right,
    stage,
    send_a,
    recv_a,
    weights,
    send_r,
    recv_sib,
    send_z,
    near_z,
    far_z,
    data,
    recv_d,
    back,
    grads,
    send_g,
    recv_g,
    load_sem,
    out_sem,
    a_sem,
    g_sem,
    sib_sem,
    near_sem,
    far_sem,
    data_sem,
    near_d_sem,
    swap_sem,
):
    n_freq, n_rtile, n_rep = dims
    n_z = n_rtile // 2
    n_slot = n_freq * n_rep
    me_f = lax.axis_index("freq")
    me_t = lax.axis_index("rtile")
    me_p = lax.axis_index("rep")
    me_slot = me_f * n_rep + me_p
    me_z = me_t // 2
    me_c = me_t % 2
    me_k = me_z % 4
    me_b = me_z // 4
    sibling = {"rtile": me_z * 2 + (1 - me_c)}
    group = model_ref.shape[1] // n_rep
    freq_local, row_tiles, col_tiles, rank_size, tile_size = right.shape[1:]

    def slot_device(slot):
        return {"freq": slot // n_rep, "rep": slot % n_rep}

    def hops(shift):
        return min(shift[0], 8 - shift[0]) + min(shift[1], 4 - shift[1])

    shifts = sorted(((dy, dx) for dy in range(8) for dx in range(4)), key=hops)[:0:-1]
    me_y = me_p * 4 + me_f // 4
    me_x = me_f % 4
    peers = []
    for dy, dx in shifts:
        y = (me_y + dy) % 8
        peers.append((y % 4 * 4 + (me_x + dx) % 4) * 2 + y // 4)

    def z_device(z):
        return {"rtile": z * 2 + me_c}

    def slots_like(send_sem, recv_sem):
        most = recv_a.at[pl.ds(0, n_slot - 1)]
        return pltpu.make_async_remote_copy(
            src_ref=most,
            dst_ref=most,
            send_sem=send_sem,
            recv_sem=recv_sem,
            device_id=sibling,
            device_id_type=MESH,
        )

    def chunks_like(count, send_sem, recv_sem):
        most = recv_sib.at[pl.ds(0, count)]
        return pltpu.make_async_remote_copy(
            src_ref=most,
            dst_ref=most,
            send_sem=send_sem,
            recv_sem=recv_sem,
            device_id=sibling,
            device_id_type=MESH,
        )

    model_load = pltpu.make_async_copy(
        model_ref.at[0, pl.ds(me_p * group, group)], traces, load_sem.at[0]
    )
    table_load = pltpu.make_async_copy(table_ref, table, load_sem.at[1])
    right_load = pltpu.make_async_copy(right_ref, right, load_sem.at[2])
    left_load = pltpu.make_async_copy(left_ref, left, load_sem.at[3])
    model_load.start()
    table_load.start()
    data_load = pltpu.make_async_copy(data_ref, data.at[me_b], load_sem.at[4])

    barrier = pltpu.get_barrier_semaphore()

    for slot in peers:
        pl.semaphore_signal(barrier, inc=1, device_id=slot_device(slot), device_id_type=MESH)
    for shift in (1, 2, 4, n_z - 4, n_z - 2, n_z - 1):
        pl.semaphore_signal(
            barrier, inc=1, device_id=z_device((me_z + shift) % n_z), device_id_type=MESH
        )
    pl.semaphore_signal(barrier, inc=1, device_id=sibling, device_id_type=MESH)

    data_load.start()
    table_load.wait()
    model_load.wait()
    right_load.start()
    left_load.start()
    bins = n_freq * freq_local
    traces_2d = traces[...].reshape(group * traces.shape[1], traces.shape[2])
    spectra = matmul(LAST, table[...], traces_2d)
    quarter = lanes((bins, 128)) // 32
    for chunk in range(group // 4):
        re = spectra[:bins, chunk * 128 : (chunk + 1) * 128]
        im = spectra[bins:, chunk * 128 : (chunk + 1) * 128]
        first = jnp.where(
            quarter == 0,
            re,
            jnp.where(
                quarter == 1,
                pltpu.roll(im, 32, 1),
                jnp.where(quarter == 2, pltpu.roll(re, 32, 1), pltpu.roll(im, 64, 1)),
            ),
        )
        second = jnp.where(
            quarter == 0,
            pltpu.roll(re, 64, 1),
            jnp.where(
                quarter == 1,
                pltpu.roll(im, 96, 1),
                jnp.where(quarter == 2, pltpu.roll(re, 96, 1), im),
            ),
        )
        stage[pl.ds(2 * chunk, bins, stride=8), :] = first
        stage[pl.ds(2 * chunk + 1, bins, stride=8), :] = second
    band = freq_local * 8
    send_a[...] = stage[...].reshape(n_freq, band, 128).astype(BF16)

    pl.semaphore_wait(barrier, n_slot - 1 + 7)

    def a_copy(target, source):
        return pltpu.make_async_remote_copy(
            src_ref=send_a.at[target // n_rep],
            dst_ref=recv_a.at[source],
            send_sem=out_sem.at[0],
            recv_sem=a_sem,
            device_id=slot_device(target),
            device_id_type=MESH,
        )

    for slot in peers:
        a_copy(slot, me_slot).start()

    def data_copy(shift, send_sem):
        return pltpu.make_async_remote_copy(
            src_ref=data.at[me_b],
            dst_ref=data.at[me_b],
            send_sem=send_sem,
            recv_sem=data_sem,
            device_id=z_device((me_z + shift) % n_z),
            device_id_type=MESH,
        )

    data_load.wait()
    data_copy(4, out_sem.at[6]).start()
    data_copy(n_z - 4, out_sem.at[6]).start()

    recv_a[me_slot] = send_a[me_f]
    right_load.wait()
    left_load.wait()

    slots_like(out_sem.at[0], a_sem).wait_recv()

    per_tile = n_slot // col_tiles
    lane_p = lanes((row_tiles * rank_size, 128))
    row_k = rows((rank_size, 128))
    low4 = rows((32, tile_size)) % 8 < 4

    def sib_copy(f):
        part = pl.ds(f * 4, 4)
        return pltpu.make_async_remote_copy(
            src_ref=send_r.at[1 - me_c, part],
            dst_ref=recv_sib.at[part],
            send_sem=out_sem.at[1],
            recv_sem=sib_sem.at[f],
            device_id=sibling,
            device_id_type=MESH,
        )

    for f in range(freq_local):
        for j in range(col_tiles):
            arrived = recv_a[j * per_tile : (j + 1) * per_tile, f * 8 : (f + 1) * 8, :]
            arrived = arrived.astype(F32).reshape(per_tile * 8, 128)
            weights[pl.ds(0, per_tile * 8, stride=2), :] = arrived
            weights[pl.ds(1, per_tile * 8, stride=2), :] = pltpu.roll(arrived, 64, 1)
            columns = weights[...].astype(BF16)
            by_re = matmul(
                PLAIN, right[0, f, :, j].reshape(row_tiles * rank_size, tile_size), columns
            )
            by_im = matmul(
                PLAIN, right[1, f, :, j].reshape(row_tiles * rank_size, tile_size), columns
            )
            projected = by_re + jnp.where(
                lane_p < 32, pltpu.roll(by_im, 96, 1), -pltpu.roll(by_im, 32, 1)
            )
            for i in range(row_tiles):
                part = projected[i * rank_size : (i + 1) * rank_size]
                back[f, i, j * rank_size : (j + 1) * rank_size, :] = jnp.where(
                    row_k < ranks_ref[f, j, i], part, 0.0
                )
        for i in range(row_tiles):
            lhs = back[f, i].T[:64].astype(BF16)
            span = slice(i * tile_size, (i + 1) * tile_size)
            by_re = matmul(PLAIN, lhs, left[0, f, i].reshape(col_tiles * rank_size, tile_size))
            by_im = matmul(PLAIN, lhs, left[1, f, i].reshape(col_tiles * rank_size, tile_size))
            out_re = by_re[:32] - by_im[32:]
            out_im = by_re[32:] + by_im[:32]
            even = jnp.where(low4, out_re, pltpu.roll(out_im, 4, 0))
            odd = jnp.where(low4, pltpu.roll(out_re, 28, 0), out_im)
            send_r[0, f * 4 : (f + 1) * 4, :, span] = even.reshape(4, 8, tile_size).astype(BF16)
            send_r[1, f * 4 : (f + 1) * 4, :, span] = odd.reshape(4, 8, tile_size).astype(BF16)
        sib_copy(f).start()

    half = send_r.shape[3] // 2
    whole = pl.ds(0, 2 * half)
    first_half = pl.ds(0, half)
    second_half = pl.ds(half, half)
    near = (
        (1, 1, 0, whole),
        (n_z - 1, 3, 1, whole),
        (2, 2, 2, first_half),
        (n_z - 2, 2, 2, second_half),
    )
    for f in range(freq_local):
        part = pl.ds(f * 4, 4)
        sib_copy(f).wait_recv()
        send_z[part] = (send_r[me_c, part].astype(F32) + recv_sib[part].astype(F32)).astype(BF16)
        for shift, ahead, place, span in near:
            pltpu.make_async_remote_copy(
                src_ref=send_z.at[f * 4 + (me_k + ahead) % 4, :, span],
                dst_ref=near_z.at[place, f, :, span],
                send_sem=out_sem.at[2],
                recv_sem=near_sem.at[f],
                device_id=z_device((me_z + shift) % n_z),
                device_id_type=MESH,
            ).start()

    far_shifts = (4, n_z - 4)
    for f in range(freq_local):
        chunks_like(3, out_sem.at[2], near_sem.at[f]).wait_recv()
        total = send_z[f * 4 + me_k].astype(F32)
        for place in range(3):
            total = total + near_z[place, f].astype(F32)
        far_z[me_b, f] = total.astype(BF16)
        for shift in far_shifts:
            pltpu.make_async_remote_copy(
                src_ref=far_z.at[me_b, f],
                dst_ref=far_z.at[me_b, f],
                send_sem=out_sem.at[3],
                recv_sem=far_sem.at[f],
                device_id=z_device((me_z + shift) % n_z),
                device_id_type=MESH,
            ).start()

    most = data.at[pl.ds(0, 2)]
    pltpu.make_async_remote_copy(
        src_ref=most,
        dst_ref=most,
        send_sem=out_sem.at[6],
        recv_sem=data_sem,
        device_id=sibling,
        device_id_type=MESH,
    ).wait()
    for f in range(freq_local):
        chunks_like(2, out_sem.at[3], far_sem.at[f]).wait_recv()
        total = far_z[0, f].astype(F32)
        for b in range(1, freq_local):
            total = total + far_z[b, f].astype(F32)
        residual_re = total[:4] - data[f, 0]
        residual_im = total[4:] - data[f, 1]
        recv_d[me_c, f * 4 + me_k] = jnp.concatenate([residual_re, residual_im], axis=0).astype(
            BF16
        )
        for shift, _, _, span in near:
            pltpu.make_async_remote_copy(
                src_ref=recv_d.at[me_c, f * 4 + me_k, :, span],
                dst_ref=recv_d.at[me_c, f * 4 + me_k, :, span],
                send_sem=out_sem.at[4],
                recv_sem=near_d_sem.at[f],
                device_id=z_device((me_z + shift) % n_z),
                device_id_type=MESH,
            ).start()
        data[f, 0] = residual_re
        data[f, 1] = residual_im
    residual_store = pltpu.make_async_copy(data.at[me_b], residual_ref, load_sem.at[5])
    residual_store.start()

    def swap_copy(f):
        part = pl.ds(f * 4, 4)
        return pltpu.make_async_remote_copy(
            src_ref=recv_d.at[me_c, part],
            dst_ref=recv_d.at[me_c, part],
            send_sem=out_sem.at[7],
            recv_sem=swap_sem.at[f],
            device_id=sibling,
            device_id_type=MESH,
        )

    for f in range(freq_local):
        chunks_like(3, out_sem.at[4], near_d_sem.at[f]).wait_recv()
        swap_copy(f).start()

    low4 = rows((32, recv_d.shape[3])) % 8 < 4
    row_k = rows((rank_size, 128))
    for f in range(freq_local):
        swap_copy(f).wait_recv()
        even = recv_d[0, f * 4 : (f + 1) * 4].astype(F32).reshape(32, -1)
        odd = recv_d[1, f * 4 : (f + 1) * 4].astype(F32).reshape(32, -1)
        mis_re = jnp.where(low4, even, pltpu.roll(odd, 4, 0))
        mis_im = jnp.where(low4, pltpu.roll(even, 28, 0), odd)
        top = jnp.concatenate([mis_re, mis_im, -mis_im, mis_re], axis=0).astype(BF16)
        low = jnp.concatenate([mis_im, -mis_re, mis_re, mis_im], axis=0).astype(BF16)
        for i in range(row_tiles):
            span = slice(i * tile_size, (i + 1) * tile_size)
            part = matmul(
                LAST, left[0, f, i].reshape(col_tiles * rank_size, tile_size), top[:, span]
            ) + matmul(
                LAST, left[1, f, i].reshape(col_tiles * rank_size, tile_size), low[:, span]
            )
            for j in range(col_tiles):
                grads[j, i * rank_size : (i + 1) * rank_size, :] = jnp.where(
                    row_k < ranks_ref[f, j, i], part[j * rank_size : (j + 1) * rank_size], 0.0
                )
        for j in range(col_tiles):
            lhs = grads[j].T.astype(BF16)
            spec_t = matmul(
                PLAIN, lhs[:64], right[0, f, :, j].reshape(row_tiles * rank_size, tile_size)
            ) + matmul(
                PLAIN, lhs[64:], right[1, f, :, j].reshape(row_tiles * rank_size, tile_size)
            )
            weights[:, :64] = spec_t.T
            even = weights[pl.ds(0, per_tile * 8, stride=2), :]
            odd = weights[pl.ds(1, per_tile * 8, stride=2), :]
            packed = jnp.where(lanes(even.shape) < 64, even, pltpu.roll(odd, 64, 1))
            send_g[j * per_tile : (j + 1) * per_tile, f * 8 : (f + 1) * 8, :] = packed.reshape(
                per_tile, 8, 128
            ).astype(BF16)

    def g_copy(target, source):
        return pltpu.make_async_remote_copy(
            src_ref=send_g.at[target],
            dst_ref=recv_g.at[source],
            send_sem=out_sem.at[5],
            recv_sem=g_sem,
            device_id=slot_device(target),
            device_id_type=MESH,
        )

    for slot in peers:
        g_copy(slot, me_slot).start()

    recv_g[me_slot] = send_g[me_slot]

    slots_like(out_sem.at[5], g_sem).wait_recv()

    for f in range(n_freq):
        both = recv_g[n_rep * f].astype(F32)
        for p in range(1, n_rep):
            both = both + recv_g[n_rep * f + p].astype(F32)
        stage[f * band : (f + 1) * band, :] = both
    for chunk in range(group // 4):
        first = stage[pl.ds(2 * chunk, bins, stride=8), :]
        second = stage[pl.ds(2 * chunk + 1, bins, stride=8), :]
        re = jnp.where(
            quarter == 0,
            first,
            jnp.where(
                quarter == 1,
                pltpu.roll(first, 96, 1),
                jnp.where(quarter == 2, pltpu.roll(second, 64, 1), pltpu.roll(second, 32, 1)),
            ),
        )
        im = jnp.where(
            quarter == 0,
            pltpu.roll(first, 96, 1),
            jnp.where(
                quarter == 1,
                pltpu.roll(first, 64, 1),
                jnp.where(quarter == 2, pltpu.roll(second, 32, 1), second),
            ),
        )
        spec_ref[:bins, chunk * 128 : (chunk + 1) * 128] = re.astype(BF16)
        spec_ref[bins:, chunk * 128 : (chunk + 1) * 128] = im.astype(BF16)

    slots_like(out_sem.at[0], a_sem).wait_send()
    slots_like(out_sem.at[5], g_sem).wait_send()
    for place, count in ((1, 12), (2, 9), (3, 6), (4, 9), (7, 12)):
        chunks_like(count, out_sem.at[place], g_sem).wait_send()
    residual_store.wait()


def traces_kernel(spec_ref, raw_ref, table_ref, residual_ref, gradient_ref, table, out, sems):
    table_load = pltpu.make_async_copy(table_ref, table, sems.at[0])
    table_load.start()
    residual_store = pltpu.make_async_copy(raw_ref, residual_ref, sems.at[1])
    residual_store.start()
    _, group, rhs_count, length = gradient_ref.shape
    steps = out.shape[0]
    part = group // steps
    lhs = spec_ref[...].astype(F32).T.astype(BF16)
    table_load.wait()
    stores = []
    for step in range(steps):
        some = lhs[step * part * rhs_count : (step + 1) * part * rhs_count]
        out[step] = matmul(PLAIN, some, table[...]).reshape(part, rhs_count, length).astype(BF16)
        store = pltpu.make_async_copy(
            out.at[step], gradient_ref.at[0, pl.ds(step * part, part)], sems.at[2 + step]
        )
        store.start()
        stores.append(store)
    residual_store.wait()
    for store in stores:
        store.wait()


def shards(dims, model, green_left, green_right, ranks, data):
    n_freq, n_rtile, n_rep = dims
    n_z = n_rtile // 2
    n_slot = n_freq * n_rep
    _, receivers, rhs_count, length = model.shape
    group = receivers // n_rep
    freq_local = ranks.shape[0]
    row_tiles, col_tiles, rank_size, tile_size = green_left.shape[2:]
    bins = n_freq * freq_local
    sources = row_tiles * tile_size
    assert (rhs_count, tile_size, group, col_tiles) == (32, 256, 16, 2)
    assert dims == (16, 24, 2)
    assert n_z == freq_local * 4 and n_slot * group == col_tiles * tile_size
    table = jnp.asarray(tables(bins, length))
    band = freq_local * 8
    raw, spec = pl.pallas_call(
        functools.partial(chain_kernel, dims),
        out_shape=(
            jax.ShapeDtypeStruct(data.shape, F32),
            jax.ShapeDtypeStruct((2 * bins, group * rhs_count), BF16),
        ),
        in_specs=[
            pl.BlockSpec(memory_space=pltpu.HBM),
            pl.BlockSpec(memory_space=pltpu.HBM),
            pl.BlockSpec(memory_space=pltpu.HBM),
            pl.BlockSpec(memory_space=pltpu.SMEM),
            pl.BlockSpec(memory_space=pltpu.HBM),
            pl.BlockSpec(memory_space=pltpu.HBM),
        ],
        out_specs=(
            pl.BlockSpec(memory_space=pltpu.HBM),
            pl.BlockSpec(memory_space=pltpu.VMEM),
        ),
        scratch_shapes=[
            pltpu.VMEM((group, rhs_count, length), BF16),
            pltpu.VMEM((2 * bins, length), BF16),
            pltpu.VMEM(green_left.shape, BF16),
            pltpu.VMEM(green_right.shape, BF16),
            pltpu.VMEM((bins * 8, 128), F32),
            pltpu.VMEM((n_freq, band, 128), BF16),
            pltpu.VMEM((n_slot, band, 128), BF16),
            pltpu.VMEM((tile_size, 128), F32),
            pltpu.VMEM((2, n_z, 8, sources), BF16),
            pltpu.VMEM((n_z, 8, sources), BF16),
            pltpu.VMEM((n_z, 8, sources), BF16),
            pltpu.VMEM((3, freq_local, 8, sources), BF16),
            pltpu.VMEM((freq_local, freq_local, 8, sources), BF16),
            pltpu.VMEM((freq_local, *data.shape), F32),
            pltpu.VMEM((2, n_z, 8, sources), BF16),
            pltpu.VMEM((freq_local, row_tiles, col_tiles * rank_size, 128), F32),
            pltpu.VMEM((col_tiles, row_tiles * rank_size, 128), F32),
            pltpu.VMEM((n_slot, band, 128), BF16),
            pltpu.VMEM((n_slot, band, 128), BF16),
            pltpu.SemaphoreType.DMA((6,)),
            pltpu.SemaphoreType.DMA((8,)),
            pltpu.SemaphoreType.DMA,
            pltpu.SemaphoreType.DMA,
            pltpu.SemaphoreType.DMA((freq_local,)),
            pltpu.SemaphoreType.DMA((freq_local,)),
            pltpu.SemaphoreType.DMA((freq_local,)),
            pltpu.SemaphoreType.DMA,
            pltpu.SemaphoreType.DMA((freq_local,)),
            pltpu.SemaphoreType.DMA((freq_local,)),
        ],
        compiler_params=pltpu.CompilerParams(
            collective_id=0, has_side_effects=True, vmem_limit_bytes=60 * 1024 * 1024
        ),
    )(model, green_left, green_right, jnp.swapaxes(ranks, 1, 2), data, table)
    steps = 4
    residual, gradient = pl.pallas_call(
        traces_kernel,
        out_shape=(
            jax.ShapeDtypeStruct(data.shape, F32),
            jax.ShapeDtypeStruct((1, group, rhs_count, length), BF16),
        ),
        in_specs=[
            pl.BlockSpec(memory_space=pltpu.VMEM),
            pl.BlockSpec(memory_space=pltpu.VMEM),
            pl.BlockSpec(memory_space=pltpu.HBM),
        ],
        out_specs=(
            pl.BlockSpec(memory_space=pltpu.HBM),
            pl.BlockSpec(memory_space=pltpu.HBM),
        ),
        scratch_shapes=[
            pltpu.VMEM((2 * bins, length), BF16),
            pltpu.VMEM((steps, group // steps, rhs_count, length), BF16),
            pltpu.SemaphoreType.DMA((2 + steps,)),
        ],
    )(spec, raw, table)
    return (residual, gradient)


def solution(mesh):
    dims = tuple(mesh.shape[name] for name in ("freq", "rtile", "rep"))
    return jax.shard_map(
        functools.partial(shards, dims),
        mesh=mesh,
        in_specs=(
            P("rtile", "freq", None, None),
            P(None, "freq", "rep", "rtile", None, None),
            P(None, "freq", "rep", "rtile", None, None),
            P("freq", "rep", "rtile"),
            P(None, ("freq", "rtile"), "rep"),
        ),
        out_specs=(P(None, ("freq", "rtile"), "rep"), P("rtile", ("freq", "rep"), None, None)),
        check_vma=False,
    )
```

```python
import functools

import jax
import jax.numpy as jnp
import ml_dtypes
import numpy as np
from jax import lax
from jax.experimental import pallas as pl
from jax.experimental.pallas import tpu as pltpu
from jax.sharding import PartitionSpec as P

MESH = pl.DeviceIdType.MESH
BF16 = jnp.bfloat16
F32 = jnp.float32
LAST = (((1,), (1,)), ((), ()))
PLAIN = (((1,), (0,)), ((), ()))


def tables(count, length):
    bins = 1 + np.arange(count, dtype=np.int64)
    phases = (bins[:, None] * np.arange(length, dtype=np.int64)[None, :] % length).astype(
        np.float32
    ) * np.float32(2.0 * np.pi / length)
    both = np.concatenate([np.cos(phases), -np.sin(phases)], axis=0)
    return both.astype(ml_dtypes.bfloat16)


def matmul(form, first, second):
    return lax.dot_general(first, second, form, preferred_element_type=F32)


def lanes(shape):
    return lax.broadcasted_iota(jnp.int32, shape, len(shape) - 1)


def rows(shape):
    return lax.broadcasted_iota(jnp.int32, shape, len(shape) - 2)


def chain_kernel(
    dims,
    model_ref,
    left_ref,
    right_ref,
    ranks_hbm,
    data_ref,
    table_ref,
    residual_ref,
    spec_ref,
    ranks_ref,
    traces,
    table,
    left,
    right,
    stage,
    send_a,
    recv_a,
    weights,
    send_r,
    recv_sib,
    send_z,
    near_z,
    far_z,
    data,
    recv_d,
    back,
    grads,
    send_g,
    recv_g,
    load_sem,
    out_sem,
    a_sem,
    g_sem,
    sib_sem,
    near_sem,
    far_sem,
    data_sem,
    near_d_sem,
    swap_sem,
):
    n_freq, n_rtile, n_rep = dims
    n_z = n_rtile // 2
    n_slot = n_freq * n_rep
    me_f = lax.axis_index("freq")
    me_t = lax.axis_index("rtile")
    me_p = lax.axis_index("rep")
    me_slot = me_f * n_rep + me_p
    me_z = me_t // 2
    me_c = me_t % 2
    me_k = me_z % 4
    me_b = me_z // 4
    sibling = {"rtile": me_z * 2 + (1 - me_c)}
    group = model_ref.shape[1] // n_rep
    freq_local, row_tiles, col_tiles, rank_size, tile_size = right.shape[1:]

    def slot_device(slot):
        return {"freq": slot // n_rep, "rep": slot % n_rep}

    def hops(shift):
        return min(shift[0], 8 - shift[0]) + min(shift[1], 4 - shift[1])

    shifts = sorted(((dy, dx) for dy in range(8) for dx in range(4)), key=hops)[:0:-1]
    me_y = me_p * 4 + me_f // 4
    me_x = me_f % 4
    peers = []
    for dy, dx in shifts:
        y = (me_y + dy) % 8
        peers.append((y % 4 * 4 + (me_x + dx) % 4) * 2 + y // 4)

    def z_device(z):
        return {"rtile": z * 2 + me_c}

    def slots_like(send_sem, recv_sem):
        most = recv_a.at[pl.ds(0, n_slot - 1)]
        return pltpu.make_async_remote_copy(
            src_ref=most,
            dst_ref=most,
            send_sem=send_sem,
            recv_sem=recv_sem,
            device_id=sibling,
            device_id_type=MESH,
        )

    def chunks_like(count, send_sem, recv_sem):
        most = recv_sib.at[pl.ds(0, count)]
        return pltpu.make_async_remote_copy(
            src_ref=most,
            dst_ref=most,
            send_sem=send_sem,
            recv_sem=recv_sem,
            device_id=sibling,
            device_id_type=MESH,
        )

    half_group = group // 2
    model_loads = [
        pltpu.make_async_copy(
            model_ref.at[0, pl.ds(me_p * group + part * half_group, half_group)],
            traces.at[pl.ds(part * half_group, half_group)],
            load_sem.at[6 + part],
        )
        for part in range(2)
    ]
    ranks_load = pltpu.make_async_copy(ranks_hbm, ranks_ref, load_sem.at[0])
    table_load = pltpu.make_async_copy(table_ref, table, load_sem.at[1])
    right_load = pltpu.make_async_copy(right_ref, right, load_sem.at[2])
    left_load = pltpu.make_async_copy(left_ref, left, load_sem.at[3])
    table_load.start()
    model_loads[0].start()
    model_loads[1].start()
    data_load = pltpu.make_async_copy(data_ref, data.at[me_b], load_sem.at[4])

    barrier = pltpu.get_barrier_semaphore()

    for slot in peers:
        pl.semaphore_signal(barrier, inc=1, device_id=slot_device(slot), device_id_type=MESH)
    for shift in (1, 2, 4, n_z - 4, n_z - 2, n_z - 1):
        pl.semaphore_signal(
            barrier, inc=1, device_id=z_device((me_z + shift) % n_z), device_id_type=MESH
        )
    pl.semaphore_signal(barrier, inc=1, device_id=sibling, device_id_type=MESH)

    data_load.start()
    right_load.start()
    left_load.start()
    ranks_load.start()

    table_load.wait()
    bins = n_freq * freq_local
    quarter = lanes((bins, 128)) // 32
    for chunk in range(group // 4):
        if chunk % 2 == 0:
            part = chunk // 2
            model_loads[part].wait()
            some = traces[part * half_group : (part + 1) * half_group]
            spectra = matmul(LAST, table[...], some.reshape(-1, traces.shape[2]))
        at = chunk % 2 * 128
        re = spectra[:bins, at : at + 128]
        im = spectra[bins:, at : at + 128]
        first = jnp.where(
            quarter == 0,
            re,
            jnp.where(
                quarter == 1,
                pltpu.roll(im, 32, 1),
                jnp.where(quarter == 2, pltpu.roll(re, 32, 1), pltpu.roll(im, 64, 1)),
            ),
        )
        second = jnp.where(
            quarter == 0,
            pltpu.roll(re, 64, 1),
            jnp.where(
                quarter == 1,
                pltpu.roll(im, 96, 1),
                jnp.where(quarter == 2, pltpu.roll(re, 96, 1), im),
            ),
        )
        stage[pl.ds(2 * chunk, bins, stride=8), :] = first
        stage[pl.ds(2 * chunk + 1, bins, stride=8), :] = second
    band = freq_local * 8
    send_a[...] = stage[...].reshape(n_freq, band, 128).astype(BF16)

    pl.semaphore_wait(barrier, n_slot - 1 + 7)

    def a_copy(target, source):
        return pltpu.make_async_remote_copy(
            src_ref=send_a.at[target // n_rep],
            dst_ref=recv_a.at[source],
            send_sem=out_sem.at[0],
            recv_sem=a_sem,
            device_id=slot_device(target),
            device_id_type=MESH,
        )

    for slot in peers:
        a_copy(slot, me_slot).start()

    def data_copy(shift, send_sem):
        return pltpu.make_async_remote_copy(
            src_ref=data.at[me_b],
            dst_ref=data.at[me_b],
            send_sem=send_sem,
            recv_sem=data_sem,
            device_id=z_device((me_z + shift) % n_z),
            device_id_type=MESH,
        )

    data_load.wait()
    data_copy(4, out_sem.at[6]).start()
    data_copy(n_z - 4, out_sem.at[6]).start()

    recv_a[me_slot] = send_a[me_f]
    right_load.wait()
    left_load.wait()
    ranks_load.wait()

    slots_like(out_sem.at[0], a_sem).wait_recv()

    per_tile = n_slot // col_tiles
    lane_p = lanes((row_tiles * rank_size, 128))
    row_k = rows((rank_size, 128))
    low4 = rows((32, tile_size)) % 8 < 4

    def sib_copy(f):
        part = pl.ds(f * 4, 4)
        return pltpu.make_async_remote_copy(
            src_ref=send_r.at[1 - me_c, part],
            dst_ref=recv_sib.at[part],
            send_sem=out_sem.at[1],
            recv_sem=sib_sem.at[f],
            device_id=sibling,
            device_id_type=MESH,
        )

    def predict(f):
        for j in range(col_tiles):
            arrived = recv_a[j * per_tile : (j + 1) * per_tile, f * 8 : (f + 1) * 8, :]
            arrived = arrived.astype(F32).reshape(per_tile * 8, 128)
            weights[pl.ds(0, per_tile * 8, stride=2), :] = arrived
            weights[pl.ds(1, per_tile * 8, stride=2), :] = pltpu.roll(arrived, 64, 1)
            columns = weights[...].astype(BF16)
            by_re = matmul(
                PLAIN, right[0, f, :, j].reshape(row_tiles * rank_size, tile_size), columns
            )
            by_im = matmul(
                PLAIN, right[1, f, :, j].reshape(row_tiles * rank_size, tile_size), columns
            )
            projected = by_re + jnp.where(
                lane_p < 32, pltpu.roll(by_im, 96, 1), -pltpu.roll(by_im, 32, 1)
            )
            for i in range(row_tiles):
                part = projected[i * rank_size : (i + 1) * rank_size]
                back[f, i, j * rank_size : (j + 1) * rank_size, :] = jnp.where(
                    row_k < ranks_ref[f, j, i], part, 0.0
                )
        for i in range(row_tiles):
            lhs = back[f, i].T[:64].astype(BF16)
            span = slice(i * tile_size, (i + 1) * tile_size)
            by_re = matmul(PLAIN, lhs, left[0, f, i].reshape(col_tiles * rank_size, tile_size))
            by_im = matmul(PLAIN, lhs, left[1, f, i].reshape(col_tiles * rank_size, tile_size))
            out_re = by_re[:32] - by_im[32:]
            out_im = by_re[32:] + by_im[:32]
            even = jnp.where(low4, out_re, pltpu.roll(out_im, 4, 0))
            odd = jnp.where(low4, pltpu.roll(out_re, 28, 0), out_im)
            send_r[0, f * 4 : (f + 1) * 4, :, span] = even.reshape(4, 8, tile_size).astype(BF16)
            send_r[1, f * 4 : (f + 1) * 4, :, span] = odd.reshape(4, 8, tile_size).astype(BF16)
        sib_copy(f).start()

    half = send_r.shape[3] // 2
    whole = pl.ds(0, 2 * half)
    first_half = pl.ds(0, half)
    second_half = pl.ds(half, half)
    near = (
        (1, 1, 0, whole),
        (n_z - 1, 3, 1, whole),
        (2, 2, 2, first_half),
        (n_z - 2, 2, 2, second_half),
    )
    def near_sends(f):
        part = pl.ds(f * 4, 4)
        sib_copy(f).wait_recv()
        send_z[part] = (send_r[me_c, part].astype(F32) + recv_sib[part].astype(F32)).astype(BF16)
        for shift, ahead, place, span in near:
            pltpu.make_async_remote_copy(
                src_ref=send_z.at[f * 4 + (me_k + ahead) % 4, :, span],
                dst_ref=near_z.at[place, f, :, span],
                send_sem=out_sem.at[2],
                recv_sem=near_sem.at[f],
                device_id=z_device((me_z + shift) % n_z),
                device_id_type=MESH,
            ).start()

    predict(0)
    for f in range(1, freq_local):
        predict(f)
        near_sends(f - 1)
    near_sends(freq_local - 1)

    far_shifts = (4, n_z - 4)
    for f in range(freq_local):
        chunks_like(3, out_sem.at[2], near_sem.at[f]).wait_recv()
        total = send_z[f * 4 + me_k].astype(F32)
        for place in range(3):
            total = total + near_z[place, f].astype(F32)
        far_z[me_b, f] = total.astype(BF16)
        for shift in far_shifts:
            pltpu.make_async_remote_copy(
                src_ref=far_z.at[me_b, f],
                dst_ref=far_z.at[me_b, f],
                send_sem=out_sem.at[3],
                recv_sem=far_sem.at[f],
                device_id=z_device((me_z + shift) % n_z),
                device_id_type=MESH,
            ).start()

    most = data.at[pl.ds(0, 2)]
    pltpu.make_async_remote_copy(
        src_ref=most,
        dst_ref=most,
        send_sem=out_sem.at[6],
        recv_sem=data_sem,
        device_id=sibling,
        device_id_type=MESH,
    ).wait()
    for f in range(freq_local):
        chunks_like(2, out_sem.at[3], far_sem.at[f]).wait_recv()
        total = far_z[0, f].astype(F32)
        for b in range(1, freq_local):
            total = total + far_z[b, f].astype(F32)
        residual_re = total[:4] - data[f, 0]
        residual_im = total[4:] - data[f, 1]
        recv_d[me_c, f * 4 + me_k] = jnp.concatenate([residual_re, residual_im], axis=0).astype(
            BF16
        )
        for shift, _, _, span in near:
            pltpu.make_async_remote_copy(
                src_ref=recv_d.at[me_c, f * 4 + me_k, :, span],
                dst_ref=recv_d.at[me_c, f * 4 + me_k, :, span],
                send_sem=out_sem.at[4],
                recv_sem=near_d_sem.at[f],
                device_id=z_device((me_z + shift) % n_z),
                device_id_type=MESH,
            ).start()
        data[f, 0] = residual_re
        data[f, 1] = residual_im
    residual_store = pltpu.make_async_copy(data.at[me_b], residual_ref, load_sem.at[5])
    residual_store.start()

    def swap_copy(f):
        part = pl.ds(f * 4, 4)
        return pltpu.make_async_remote_copy(
            src_ref=recv_d.at[me_c, part],
            dst_ref=recv_d.at[me_c, part],
            send_sem=out_sem.at[7],
            recv_sem=swap_sem.at[f],
            device_id=sibling,
            device_id_type=MESH,
        )

    for f in range(freq_local):
        chunks_like(3, out_sem.at[4], near_d_sem.at[f]).wait_recv()
        swap_copy(f).start()

    low4 = rows((32, recv_d.shape[3])) % 8 < 4
    row_k = rows((rank_size, 128))
    for f in range(freq_local):
        swap_copy(f).wait_recv()
        even = recv_d[0, f * 4 : (f + 1) * 4].astype(F32).reshape(32, -1)
        odd = recv_d[1, f * 4 : (f + 1) * 4].astype(F32).reshape(32, -1)
        mis_re = jnp.where(low4, even, pltpu.roll(odd, 4, 0))
        mis_im = jnp.where(low4, pltpu.roll(even, 28, 0), odd)
        top = jnp.concatenate([mis_re, mis_im, -mis_im, mis_re], axis=0).astype(BF16)
        low = jnp.concatenate([mis_im, -mis_re, mis_re, mis_im], axis=0).astype(BF16)
        for i in range(row_tiles):
            span = slice(i * tile_size, (i + 1) * tile_size)
            part = matmul(
                LAST, left[0, f, i].reshape(col_tiles * rank_size, tile_size), top[:, span]
            ) + matmul(
                LAST, left[1, f, i].reshape(col_tiles * rank_size, tile_size), low[:, span]
            )
            for j in range(col_tiles):
                grads[j, i * rank_size : (i + 1) * rank_size, :] = jnp.where(
                    row_k < ranks_ref[f, j, i], part[j * rank_size : (j + 1) * rank_size], 0.0
                )
        for j in range(col_tiles):
            lhs = grads[j].T.astype(BF16)
            spec_t = matmul(
                PLAIN, lhs[:64], right[0, f, :, j].reshape(row_tiles * rank_size, tile_size)
            ) + matmul(
                PLAIN, lhs[64:], right[1, f, :, j].reshape(row_tiles * rank_size, tile_size)
            )
            weights[:, :64] = spec_t.T
            even = weights[pl.ds(0, per_tile * 8, stride=2), :]
            odd = weights[pl.ds(1, per_tile * 8, stride=2), :]
            packed = jnp.where(lanes(even.shape) < 64, even, pltpu.roll(odd, 64, 1))
            send_g[j * per_tile : (j + 1) * per_tile, f * 8 : (f + 1) * 8, :] = packed.reshape(
                per_tile, 8, 128
            ).astype(BF16)

    def g_copy(target, source):
        return pltpu.make_async_remote_copy(
            src_ref=send_g.at[target],
            dst_ref=recv_g.at[source],
            send_sem=out_sem.at[5],
            recv_sem=g_sem,
            device_id=slot_device(target),
            device_id_type=MESH,
        )

    for slot in peers:
        g_copy(slot, me_slot).start()

    recv_g[me_slot] = send_g[me_slot]

    slots_like(out_sem.at[5], g_sem).wait_recv()

    for f in range(n_freq):
        both = recv_g[n_rep * f].astype(F32)
        for p in range(1, n_rep):
            both = both + recv_g[n_rep * f + p].astype(F32)
        stage[f * band : (f + 1) * band, :] = both
    for chunk in range(group // 4):
        first = stage[pl.ds(2 * chunk, bins, stride=8), :]
        second = stage[pl.ds(2 * chunk + 1, bins, stride=8), :]
        re = jnp.where(
            quarter == 0,
            first,
            jnp.where(
                quarter == 1,
                pltpu.roll(first, 96, 1),
                jnp.where(quarter == 2, pltpu.roll(second, 64, 1), pltpu.roll(second, 32, 1)),
            ),
        )
        im = jnp.where(
            quarter == 0,
            pltpu.roll(first, 96, 1),
            jnp.where(
                quarter == 1,
                pltpu.roll(first, 64, 1),
                jnp.where(quarter == 2, pltpu.roll(second, 32, 1), second),
            ),
        )
        spec_ref[:bins, chunk * 128 : (chunk + 1) * 128] = re.astype(BF16)
        spec_ref[bins:, chunk * 128 : (chunk + 1) * 128] = im.astype(BF16)

    slots_like(out_sem.at[0], a_sem).wait_send()
    slots_like(out_sem.at[5], g_sem).wait_send()
    for place, count in ((1, 12), (2, 9), (3, 6), (4, 9), (7, 12)):
        chunks_like(count, out_sem.at[place], g_sem).wait_send()
    residual_store.wait()


def traces_kernel(
    spec_ref, raw_ref, table_ref, residual_ref, gradient_ref, spec, table, raw, out, sems
):
    spec_load = pltpu.make_async_copy(spec_ref, spec, sems.at[0])
    table_load = pltpu.make_async_copy(table_ref, table, sems.at[1])
    raw_load = pltpu.make_async_copy(raw_ref, raw, sems.at[2])
    residual_store = pltpu.make_async_copy(raw, residual_ref, sems.at[3])
    spec_load.start()
    table_load.start()
    raw_load.start()
    _, group, rhs_count, length = gradient_ref.shape
    steps = out.shape[0]
    part = group // steps
    spec_load.wait()
    lhs = spec[...].astype(F32).T.astype(BF16)
    table_load.wait()
    raw_load.wait()
    residual_store.start()
    stores = []
    for step in range(steps):
        some = lhs[step * part * rhs_count : (step + 1) * part * rhs_count]
        out[step] = matmul(PLAIN, some, table[...]).reshape(part, rhs_count, length).astype(BF16)
        store = pltpu.make_async_copy(
            out.at[step], gradient_ref.at[0, pl.ds(step * part, part)], sems.at[4 + step]
        )
        store.start()
        stores.append(store)
    residual_store.wait()
    for store in stores:
        store.wait()


def shards(dims, model, green_left, green_right, ranks, data):
    n_freq, n_rtile, n_rep = dims
    n_z = n_rtile // 2
    n_slot = n_freq * n_rep
    _, receivers, rhs_count, length = model.shape
    group = receivers // n_rep
    freq_local = ranks.shape[0]
    row_tiles, col_tiles, rank_size, tile_size = green_left.shape[2:]
    bins = n_freq * freq_local
    sources = row_tiles * tile_size
    assert (rhs_count, tile_size, group, col_tiles) == (32, 256, 16, 2)
    assert dims == (16, 24, 2)
    assert n_z == freq_local * 4 and n_slot * group == col_tiles * tile_size
    table = jnp.asarray(tables(bins, length))
    band = freq_local * 8
    raw, spec = pl.pallas_call(
        functools.partial(chain_kernel, dims),
        out_shape=(
            jax.ShapeDtypeStruct(data.shape, F32),
            jax.ShapeDtypeStruct((2 * bins, group * rhs_count), BF16),
        ),
        in_specs=[
            pl.BlockSpec(memory_space=pltpu.HBM),
            pl.BlockSpec(memory_space=pltpu.HBM),
            pl.BlockSpec(memory_space=pltpu.HBM),
            pl.BlockSpec(memory_space=pltpu.HBM),
            pl.BlockSpec(memory_space=pltpu.HBM),
            pl.BlockSpec(memory_space=pltpu.HBM),
        ],
        out_specs=(
            pl.BlockSpec(memory_space=pltpu.HBM),
            pl.BlockSpec(memory_space=pltpu.VMEM),
        ),
        scratch_shapes=[
            pltpu.SMEM((freq_local, col_tiles, row_tiles), jnp.int32),
            pltpu.VMEM((group, rhs_count, length), BF16),
            pltpu.VMEM((2 * bins, length), BF16),
            pltpu.VMEM(green_left.shape, BF16),
            pltpu.VMEM(green_right.shape, BF16),
            pltpu.VMEM((bins * 8, 128), F32),
            pltpu.VMEM((n_freq, band, 128), BF16),
            pltpu.VMEM((n_slot, band, 128), BF16),
            pltpu.VMEM((tile_size, 128), F32),
            pltpu.VMEM((2, n_z, 8, sources), BF16),
            pltpu.VMEM((n_z, 8, sources), BF16),
            pltpu.VMEM((n_z, 8, sources), BF16),
            pltpu.VMEM((3, freq_local, 8, sources), BF16),
            pltpu.VMEM((freq_local, freq_local, 8, sources), BF16),
            pltpu.VMEM((freq_local, *data.shape), F32),
            pltpu.VMEM((2, n_z, 8, sources), BF16),
            pltpu.VMEM((freq_local, row_tiles, col_tiles * rank_size, 128), F32),
            pltpu.VMEM((col_tiles, row_tiles * rank_size, 128), F32),
            pltpu.VMEM((n_slot, band, 128), BF16),
            pltpu.VMEM((n_slot, band, 128), BF16),
            pltpu.SemaphoreType.DMA((8,)),
            pltpu.SemaphoreType.DMA((8,)),
            pltpu.SemaphoreType.DMA,
            pltpu.SemaphoreType.DMA,
            pltpu.SemaphoreType.DMA((freq_local,)),
            pltpu.SemaphoreType.DMA((freq_local,)),
            pltpu.SemaphoreType.DMA((freq_local,)),
            pltpu.SemaphoreType.DMA,
            pltpu.SemaphoreType.DMA((freq_local,)),
            pltpu.SemaphoreType.DMA((freq_local,)),
        ],
        compiler_params=pltpu.CompilerParams(
            collective_id=0, has_side_effects=True, vmem_limit_bytes=60 * 1024 * 1024
        ),
    )(model, green_left, green_right, jnp.swapaxes(ranks, 1, 2), data, table)
    steps = 4
    residual, gradient = pl.pallas_call(
        traces_kernel,
        out_shape=(
            jax.ShapeDtypeStruct(data.shape, F32),
            jax.ShapeDtypeStruct((1, group, rhs_count, length), BF16),
        ),
        in_specs=[
            pl.BlockSpec(memory_space=pltpu.HBM),
            pl.BlockSpec(memory_space=pltpu.HBM),
            pl.BlockSpec(memory_space=pltpu.HBM),
        ],
        out_specs=(
            pl.BlockSpec(memory_space=pltpu.HBM),
            pl.BlockSpec(memory_space=pltpu.HBM),
        ),
        scratch_shapes=[
            pltpu.VMEM((2 * bins, group * rhs_count), BF16),
            pltpu.VMEM((2 * bins, length), BF16),
            pltpu.VMEM(data.shape, F32),
            pltpu.VMEM((steps, group // steps, rhs_count, length), BF16),
            pltpu.SemaphoreType.DMA((4 + steps,)),
        ],
        compiler_params=pltpu.CompilerParams(vmem_limit_bytes=60 * 1024 * 1024),
    )(spec, raw, table)
    return (residual, gradient)


def solution(mesh):
    dims = tuple(mesh.shape[name] for name in ("freq", "rtile", "rep"))
    return jax.shard_map(
        functools.partial(shards, dims),
        mesh=mesh,
        in_specs=(
            P("rtile", "freq", None, None),
            P(None, "freq", "rep", "rtile", None, None),
            P(None, "freq", "rep", "rtile", None, None),
            P("freq", "rep", "rtile"),
            P(None, ("freq", "rtile"), "rep"),
        ),
        out_specs=(P(None, ("freq", "rtile"), "rep"), P("rtile", ("freq", "rep"), None, None)),
        check_vma=False,
    )
```

```python
import functools

import jax
import jax.numpy as jnp
import ml_dtypes
import numpy as np
from jax import lax
from jax.experimental import pallas as pl
from jax.experimental.pallas import tpu as pltpu
from jax.sharding import PartitionSpec as P

MESH = pl.DeviceIdType.MESH
BF16 = jnp.bfloat16
F32 = jnp.float32
LAST = (((1,), (1,)), ((), ()))
PLAIN = (((1,), (0,)), ((), ()))


def tables(count, length):
    bins = 1 + np.arange(count, dtype=np.int64)
    phases = (bins[:, None] * np.arange(length, dtype=np.int64)[None, :] % length).astype(
        np.float32
    ) * np.float32(2.0 * np.pi / length)
    both = np.concatenate([np.cos(phases), -np.sin(phases)], axis=0)
    return both.astype(ml_dtypes.bfloat16)


def matmul(form, first, second):
    return lax.dot_general(first, second, form, preferred_element_type=F32)


def lanes(shape):
    return lax.broadcasted_iota(jnp.int32, shape, len(shape) - 1)


def rows(shape):
    return lax.broadcasted_iota(jnp.int32, shape, len(shape) - 2)


def chain_kernel(
    dims,
    model_ref,
    left_ref,
    right_ref,
    ranks_hbm,
    data_ref,
    table_ref,
    residual_ref,
    spec_ref,
    ranks_ref,
    traces,
    table,
    left,
    right,
    stage,
    send_a,
    recv_a,
    weights,
    send_r,
    recv_sib,
    send_z,
    near_z,
    far_z,
    data,
    recv_d,
    back,
    grads,
    send_g,
    recv_g,
    load_sem,
    out_sem,
    a_sem,
    g_sem,
    sib_sem,
    near_sem,
    far_sem,
    data_sem,
    near_d_sem,
    swap_sem,
):
    n_freq, n_rtile, n_rep = dims
    n_z = n_rtile // 2
    n_slot = n_freq * n_rep
    me_f = lax.axis_index("freq")
    me_t = lax.axis_index("rtile")
    me_p = lax.axis_index("rep")
    me_slot = me_f * n_rep + me_p
    me_z = me_t // 2
    me_c = me_t % 2
    me_k = me_z % 4
    me_b = me_z // 4
    sibling = {"rtile": me_z * 2 + (1 - me_c)}
    group = model_ref.shape[1] // n_rep
    freq_local, row_tiles, col_tiles, rank_size, tile_size = right.shape[1:]

    def slot_device(slot):
        return {"freq": slot // n_rep, "rep": slot % n_rep}

    def hops(shift):
        return min(shift[0], 8 - shift[0]) + min(shift[1], 4 - shift[1])

    shifts = sorted(((dy, dx) for dy in range(8) for dx in range(4)), key=hops)[:0:-1]
    me_y = me_p * 4 + me_f // 4
    me_x = me_f % 4
    peers = []
    for dy, dx in shifts:
        y = (me_y + dy) % 8
        peers.append((y % 4 * 4 + (me_x + dx) % 4) * 2 + y // 4)

    def z_device(z):
        return {"rtile": z * 2 + me_c}

    def slots_like(send_sem, recv_sem):
        most = recv_a.at[pl.ds(0, n_slot - 1)]
        return pltpu.make_async_remote_copy(
            src_ref=most,
            dst_ref=most,
            send_sem=send_sem,
            recv_sem=recv_sem,
            device_id=sibling,
            device_id_type=MESH,
        )

    def chunks_like(count, send_sem, recv_sem):
        most = recv_sib.at[pl.ds(0, count)]
        return pltpu.make_async_remote_copy(
            src_ref=most,
            dst_ref=most,
            send_sem=send_sem,
            recv_sem=recv_sem,
            device_id=sibling,
            device_id_type=MESH,
        )

    half_group = group // 2
    model_loads = [
        pltpu.make_async_copy(
            model_ref.at[0, pl.ds(me_p * group + part * half_group, half_group)],
            traces.at[pl.ds(part * half_group, half_group)],
            load_sem.at[6 + part],
        )
        for part in range(2)
    ]
    ranks_load = pltpu.make_async_copy(ranks_hbm, ranks_ref, load_sem.at[0])
    table_load = pltpu.make_async_copy(table_ref, table, load_sem.at[1])
    right_load = pltpu.make_async_copy(right_ref, right, load_sem.at[2])
    left_load = pltpu.make_async_copy(left_ref, left, load_sem.at[3])
    table_load.start()
    model_loads[0].start()
    model_loads[1].start()
    data_load = pltpu.make_async_copy(data_ref, data.at[me_b], load_sem.at[4])

    barrier = pltpu.get_barrier_semaphore()

    for slot in peers:
        pl.semaphore_signal(barrier, inc=1, device_id=slot_device(slot), device_id_type=MESH)
    for shift in (1, 2, 4, n_z - 4, n_z - 2, n_z - 1):
        pl.semaphore_signal(
            barrier, inc=1, device_id=z_device((me_z + shift) % n_z), device_id_type=MESH
        )
    pl.semaphore_signal(barrier, inc=1, device_id=sibling, device_id_type=MESH)

    data_load.start()
    right_load.start()
    left_load.start()
    ranks_load.start()

    table_load.wait()
    bins = n_freq * freq_local
    quarter = lanes((bins, 128)) // 32
    for chunk in range(group // 4):
        if chunk % 2 == 0:
            part = chunk // 2
            model_loads[part].wait()
            some = traces[part * half_group : (part + 1) * half_group]
            spectra = matmul(LAST, table[...], some.reshape(-1, traces.shape[2]))
        at = chunk % 2 * 128
        re = spectra[:bins, at : at + 128]
        im = spectra[bins:, at : at + 128]
        first = jnp.where(
            quarter == 0,
            re,
            jnp.where(
                quarter == 1,
                pltpu.roll(im, 32, 1),
                jnp.where(quarter == 2, pltpu.roll(re, 32, 1), pltpu.roll(im, 64, 1)),
            ),
        )
        second = jnp.where(
            quarter == 0,
            pltpu.roll(re, 64, 1),
            jnp.where(
                quarter == 1,
                pltpu.roll(im, 96, 1),
                jnp.where(quarter == 2, pltpu.roll(re, 96, 1), im),
            ),
        )
        stage[pl.ds(2 * chunk, bins, stride=8), :] = first
        stage[pl.ds(2 * chunk + 1, bins, stride=8), :] = second
    band = freq_local * 8
    send_a[...] = stage[...].reshape(n_freq, band, 128).astype(BF16)

    pl.semaphore_wait(barrier, n_slot - 1 + 7)

    def a_copy(target, source):
        return pltpu.make_async_remote_copy(
            src_ref=send_a.at[target // n_rep],
            dst_ref=recv_a.at[source],
            send_sem=out_sem.at[0],
            recv_sem=a_sem,
            device_id=slot_device(target),
            device_id_type=MESH,
        )

    for slot in peers:
        a_copy(slot, me_slot).start()

    def data_copy(shift, send_sem):
        return pltpu.make_async_remote_copy(
            src_ref=data.at[me_b],
            dst_ref=data.at[me_b],
            send_sem=send_sem,
            recv_sem=data_sem,
            device_id=z_device((me_z + shift) % n_z),
            device_id_type=MESH,
        )

    data_load.wait()
    data_copy(4, out_sem.at[6]).start()
    data_copy(n_z - 4, out_sem.at[6]).start()

    recv_a[me_slot] = send_a[me_f]
    right_load.wait()
    left_load.wait()
    ranks_load.wait()

    slots_like(out_sem.at[0], a_sem).wait_recv()

    per_tile = n_slot // col_tiles
    lane_p = lanes((row_tiles * rank_size, 128))
    row_k = rows((rank_size, 128))
    low4 = rows((32, tile_size)) % 8 < 4

    def sib_copy(f):
        part = pl.ds(f * 4, 4)
        return pltpu.make_async_remote_copy(
            src_ref=send_r.at[1 - me_c, part],
            dst_ref=recv_sib.at[part],
            send_sem=out_sem.at[1],
            recv_sem=sib_sem.at[f],
            device_id=sibling,
            device_id_type=MESH,
        )

    def predict(f):
        for j in range(col_tiles):
            arrived = recv_a[j * per_tile : (j + 1) * per_tile, f * 8 : (f + 1) * 8, :]
            arrived = arrived.astype(F32).reshape(per_tile * 8, 128)
            weights[pl.ds(0, per_tile * 8, stride=2), :] = arrived
            weights[pl.ds(1, per_tile * 8, stride=2), :] = pltpu.roll(arrived, 64, 1)
            columns = weights[...].astype(BF16)
            by_re = matmul(
                PLAIN, right[0, f, :, j].reshape(row_tiles * rank_size, tile_size), columns
            )
            by_im = matmul(
                PLAIN, right[1, f, :, j].reshape(row_tiles * rank_size, tile_size), columns
            )
            projected = by_re + jnp.where(
                lane_p < 32, pltpu.roll(by_im, 96, 1), -pltpu.roll(by_im, 32, 1)
            )
            for i in range(row_tiles):
                part = projected[i * rank_size : (i + 1) * rank_size]
                back[f, i, j * rank_size : (j + 1) * rank_size, :] = jnp.where(
                    row_k < ranks_ref[f, j, i], part, 0.0
                )
        for i in range(row_tiles):
            lhs = back[f, i].T[:64].astype(BF16)
            span = slice(i * tile_size, (i + 1) * tile_size)
            by_re = matmul(PLAIN, lhs, left[0, f, i].reshape(col_tiles * rank_size, tile_size))
            by_im = matmul(PLAIN, lhs, left[1, f, i].reshape(col_tiles * rank_size, tile_size))
            out_re = by_re[:32] - by_im[32:]
            out_im = by_re[32:] + by_im[:32]
            even = jnp.where(low4, out_re, pltpu.roll(out_im, 4, 0))
            odd = jnp.where(low4, pltpu.roll(out_re, 28, 0), out_im)
            send_r[0, f * 4 : (f + 1) * 4, :, span] = even.reshape(4, 8, tile_size).astype(BF16)
            send_r[1, f * 4 : (f + 1) * 4, :, span] = odd.reshape(4, 8, tile_size).astype(BF16)
        sib_copy(f).start()

    half = send_r.shape[3] // 2
    whole = pl.ds(0, 2 * half)
    first_half = pl.ds(0, half)
    second_half = pl.ds(half, half)
    near = (
        (2, 2, 2, first_half),
        (n_z - 2, 2, 2, second_half),
        (1, 1, 0, whole),
        (n_z - 1, 3, 1, whole),
    )
    def near_sends(f):
        part = pl.ds(f * 4, 4)
        sib_copy(f).wait_recv()
        send_z[part] = (send_r[me_c, part].astype(F32) + recv_sib[part].astype(F32)).astype(BF16)
        for shift, ahead, place, span in near:
            pltpu.make_async_remote_copy(
                src_ref=send_z.at[f * 4 + (me_k + ahead) % 4, :, span],
                dst_ref=near_z.at[place, f, :, span],
                send_sem=out_sem.at[2],
                recv_sem=near_sem.at[f],
                device_id=z_device((me_z + shift) % n_z),
                device_id_type=MESH,
            ).start()

    predict(0)
    for f in range(1, freq_local):
        predict(f)
        near_sends(f - 1)
    near_sends(freq_local - 1)

    far_shifts = (4, n_z - 4)
    for f in range(freq_local):
        chunks_like(3, out_sem.at[2], near_sem.at[f]).wait_recv()
        total = send_z[f * 4 + me_k].astype(F32)
        for place in range(3):
            total = total + near_z[place, f].astype(F32)
        far_z[me_b, f] = total.astype(BF16)
        for shift in far_shifts:
            pltpu.make_async_remote_copy(
                src_ref=far_z.at[me_b, f],
                dst_ref=far_z.at[me_b, f],
                send_sem=out_sem.at[3],
                recv_sem=far_sem.at[f],
                device_id=z_device((me_z + shift) % n_z),
                device_id_type=MESH,
            ).start()

    most = data.at[pl.ds(0, 2)]
    pltpu.make_async_remote_copy(
        src_ref=most,
        dst_ref=most,
        send_sem=out_sem.at[6],
        recv_sem=data_sem,
        device_id=sibling,
        device_id_type=MESH,
    ).wait()
    for f in range(freq_local):
        chunks_like(2, out_sem.at[3], far_sem.at[f]).wait_recv()
        total = far_z[0, f].astype(F32)
        for b in range(1, freq_local):
            total = total + far_z[b, f].astype(F32)
        residual_re = total[:4] - data[f, 0]
        residual_im = total[4:] - data[f, 1]
        recv_d[me_c, f * 4 + me_k] = jnp.concatenate([residual_re, residual_im], axis=0).astype(
            BF16
        )
        for shift, _, _, span in near:
            pltpu.make_async_remote_copy(
                src_ref=recv_d.at[me_c, f * 4 + me_k, :, span],
                dst_ref=recv_d.at[me_c, f * 4 + me_k, :, span],
                send_sem=out_sem.at[4],
                recv_sem=near_d_sem.at[f],
                device_id=z_device((me_z + shift) % n_z),
                device_id_type=MESH,
            ).start()
        data[f, 0] = residual_re
        data[f, 1] = residual_im
    residual_store = pltpu.make_async_copy(data.at[me_b], residual_ref, load_sem.at[5])
    residual_store.start()

    def swap_copy(f):
        part = pl.ds(f * 4, 4)
        return pltpu.make_async_remote_copy(
            src_ref=recv_d.at[me_c, part],
            dst_ref=recv_d.at[me_c, part],
            send_sem=out_sem.at[7],
            recv_sem=swap_sem.at[f],
            device_id=sibling,
            device_id_type=MESH,
        )

    for f in range(freq_local):
        chunks_like(3, out_sem.at[4], near_d_sem.at[f]).wait_recv()
        swap_copy(f).start()

    low4 = rows((32, recv_d.shape[3])) % 8 < 4
    row_k = rows((rank_size, 128))
    for f in range(freq_local):
        swap_copy(f).wait_recv()
        even = recv_d[0, f * 4 : (f + 1) * 4].astype(F32).reshape(32, -1)
        odd = recv_d[1, f * 4 : (f + 1) * 4].astype(F32).reshape(32, -1)
        mis_re = jnp.where(low4, even, pltpu.roll(odd, 4, 0))
        mis_im = jnp.where(low4, pltpu.roll(even, 28, 0), odd)
        top = jnp.concatenate([mis_re, mis_im, -mis_im, mis_re], axis=0).astype(BF16)
        low = jnp.concatenate([mis_im, -mis_re, mis_re, mis_im], axis=0).astype(BF16)
        for i in range(row_tiles):
            span = slice(i * tile_size, (i + 1) * tile_size)
            part = matmul(
                LAST, left[0, f, i].reshape(col_tiles * rank_size, tile_size), top[:, span]
            ) + matmul(
                LAST, left[1, f, i].reshape(col_tiles * rank_size, tile_size), low[:, span]
            )
            for j in range(col_tiles):
                grads[j, i * rank_size : (i + 1) * rank_size, :] = jnp.where(
                    row_k < ranks_ref[f, j, i], part[j * rank_size : (j + 1) * rank_size], 0.0
                )
        for j in range(col_tiles):
            lhs = grads[j].T.astype(BF16)
            spec_t = matmul(
                PLAIN, lhs[:64], right[0, f, :, j].reshape(row_tiles * rank_size, tile_size)
            ) + matmul(
                PLAIN, lhs[64:], right[1, f, :, j].reshape(row_tiles * rank_size, tile_size)
            )
            weights[:, :64] = spec_t.T
            even = weights[pl.ds(0, per_tile * 8, stride=2), :]
            odd = weights[pl.ds(1, per_tile * 8, stride=2), :]
            packed = jnp.where(lanes(even.shape) < 64, even, pltpu.roll(odd, 64, 1))
            send_g[j * per_tile : (j + 1) * per_tile, f * 8 : (f + 1) * 8, :] = packed.reshape(
                per_tile, 8, 128
            ).astype(BF16)

    def g_copy(target, source):
        return pltpu.make_async_remote_copy(
            src_ref=send_g.at[target],
            dst_ref=recv_g.at[source],
            send_sem=out_sem.at[5],
            recv_sem=g_sem,
            device_id=slot_device(target),
            device_id_type=MESH,
        )

    for slot in peers:
        g_copy(slot, me_slot).start()

    recv_g[me_slot] = send_g[me_slot]

    slots_like(out_sem.at[5], g_sem).wait_recv()

    for f in range(n_freq):
        both = recv_g[n_rep * f].astype(F32)
        for p in range(1, n_rep):
            both = both + recv_g[n_rep * f + p].astype(F32)
        stage[f * band : (f + 1) * band, :] = both
    for chunk in range(group // 4):
        first = stage[pl.ds(2 * chunk, bins, stride=8), :]
        second = stage[pl.ds(2 * chunk + 1, bins, stride=8), :]
        re = jnp.where(
            quarter == 0,
            first,
            jnp.where(
                quarter == 1,
                pltpu.roll(first, 96, 1),
                jnp.where(quarter == 2, pltpu.roll(second, 64, 1), pltpu.roll(second, 32, 1)),
            ),
        )
        im = jnp.where(
            quarter == 0,
            pltpu.roll(first, 96, 1),
            jnp.where(
                quarter == 1,
                pltpu.roll(first, 64, 1),
                jnp.where(quarter == 2, pltpu.roll(second, 32, 1), second),
            ),
        )
        spec_ref[:bins, chunk * 128 : (chunk + 1) * 128] = re.astype(BF16)
        spec_ref[bins:, chunk * 128 : (chunk + 1) * 128] = im.astype(BF16)

    slots_like(out_sem.at[0], a_sem).wait_send()
    slots_like(out_sem.at[5], g_sem).wait_send()
    for place, count in ((1, 12), (2, 9), (3, 6), (4, 9), (7, 12)):
        chunks_like(count, out_sem.at[place], g_sem).wait_send()
    residual_store.wait()


def traces_kernel(
    spec_ref, raw_ref, table_ref, residual_ref, gradient_ref, spec, table, raw, out, sems
):
    spec_load = pltpu.make_async_copy(spec_ref, spec, sems.at[0])
    table_load = pltpu.make_async_copy(table_ref, table, sems.at[1])
    raw_load = pltpu.make_async_copy(raw_ref, raw, sems.at[2])
    residual_store = pltpu.make_async_copy(raw, residual_ref, sems.at[3])
    spec_load.start()
    table_load.start()
    raw_load.start()
    _, group, rhs_count, length = gradient_ref.shape
    steps = out.shape[0]
    part = group // steps
    spec_load.wait()
    lhs = spec[...].astype(F32).T.astype(BF16)
    table_load.wait()
    raw_load.wait()
    residual_store.start()
    stores = []
    for step in range(steps):
        some = lhs[step * part * rhs_count : (step + 1) * part * rhs_count]
        out[step] = matmul(PLAIN, some, table[...]).reshape(part, rhs_count, length).astype(BF16)
        store = pltpu.make_async_copy(
            out.at[step], gradient_ref.at[0, pl.ds(step * part, part)], sems.at[4 + step]
        )
        store.start()
        stores.append(store)
    residual_store.wait()
    for store in stores:
        store.wait()


def shards(dims, model, green_left, green_right, ranks, data):
    n_freq, n_rtile, n_rep = dims
    n_z = n_rtile // 2
    n_slot = n_freq * n_rep
    _, receivers, rhs_count, length = model.shape
    group = receivers // n_rep
    freq_local = ranks.shape[0]
    row_tiles, col_tiles, rank_size, tile_size = green_left.shape[2:]
    bins = n_freq * freq_local
    sources = row_tiles * tile_size
    assert (rhs_count, tile_size, group, col_tiles) == (32, 256, 16, 2)
    assert dims == (16, 24, 2)
    assert n_z == freq_local * 4 and n_slot * group == col_tiles * tile_size
    table = jnp.asarray(tables(bins, length))
    band = freq_local * 8
    raw, spec = pl.pallas_call(
        functools.partial(chain_kernel, dims),
        out_shape=(
            jax.ShapeDtypeStruct(data.shape, F32),
            jax.ShapeDtypeStruct((2 * bins, group * rhs_count), BF16),
        ),
        in_specs=[
            pl.BlockSpec(memory_space=pltpu.HBM),
            pl.BlockSpec(memory_space=pltpu.HBM),
            pl.BlockSpec(memory_space=pltpu.HBM),
            pl.BlockSpec(memory_space=pltpu.HBM),
            pl.BlockSpec(memory_space=pltpu.HBM),
            pl.BlockSpec(memory_space=pltpu.HBM),
        ],
        out_specs=(
            pl.BlockSpec(memory_space=pltpu.HBM),
            pl.BlockSpec(memory_space=pltpu.VMEM),
        ),
        scratch_shapes=[
            pltpu.SMEM((freq_local, col_tiles, row_tiles), jnp.int32),
            pltpu.VMEM((group, rhs_count, length), BF16),
            pltpu.VMEM((2 * bins, length), BF16),
            pltpu.VMEM(green_left.shape, BF16),
            pltpu.VMEM(green_right.shape, BF16),
            pltpu.VMEM((bins * 8, 128), F32),
            pltpu.VMEM((n_freq, band, 128), BF16),
            pltpu.VMEM((n_slot, band, 128), BF16),
            pltpu.VMEM((tile_size, 128), F32),
            pltpu.VMEM((2, n_z, 8, sources), BF16),
            pltpu.VMEM((n_z, 8, sources), BF16),
            pltpu.VMEM((n_z, 8, sources), BF16),
            pltpu.VMEM((3, freq_local, 8, sources), BF16),
            pltpu.VMEM((freq_local, freq_local, 8, sources), BF16),
            pltpu.VMEM((freq_local, *data.shape), F32),
            pltpu.VMEM((2, n_z, 8, sources), BF16),
            pltpu.VMEM((freq_local, row_tiles, col_tiles * rank_size, 128), F32),
            pltpu.VMEM((col_tiles, row_tiles * rank_size, 128), F32),
            pltpu.VMEM((n_slot, band, 128), BF16),
            pltpu.VMEM((n_slot, band, 128), BF16),
            pltpu.SemaphoreType.DMA((8,)),
            pltpu.SemaphoreType.DMA((8,)),
            pltpu.SemaphoreType.DMA,
            pltpu.SemaphoreType.DMA,
            pltpu.SemaphoreType.DMA((freq_local,)),
            pltpu.SemaphoreType.DMA((freq_local,)),
            pltpu.SemaphoreType.DMA((freq_local,)),
            pltpu.SemaphoreType.DMA,
            pltpu.SemaphoreType.DMA((freq_local,)),
            pltpu.SemaphoreType.DMA((freq_local,)),
        ],
        compiler_params=pltpu.CompilerParams(
            collective_id=0, has_side_effects=True, vmem_limit_bytes=60 * 1024 * 1024
        ),
    )(model, green_left, green_right, jnp.swapaxes(ranks, 1, 2), data, table)
    steps = 4
    residual, gradient = pl.pallas_call(
        traces_kernel,
        out_shape=(
            jax.ShapeDtypeStruct(data.shape, F32),
            jax.ShapeDtypeStruct((1, group, rhs_count, length), BF16),
        ),
        in_specs=[
            pl.BlockSpec(memory_space=pltpu.HBM),
            pl.BlockSpec(memory_space=pltpu.HBM),
            pl.BlockSpec(memory_space=pltpu.HBM),
        ],
        out_specs=(
            pl.BlockSpec(memory_space=pltpu.HBM),
            pl.BlockSpec(memory_space=pltpu.HBM),
        ),
        scratch_shapes=[
            pltpu.VMEM((2 * bins, group * rhs_count), BF16),
            pltpu.VMEM((2 * bins, length), BF16),
            pltpu.VMEM(data.shape, F32),
            pltpu.VMEM((steps, group // steps, rhs_count, length), BF16),
            pltpu.SemaphoreType.DMA((4 + steps,)),
        ],
        compiler_params=pltpu.CompilerParams(vmem_limit_bytes=60 * 1024 * 1024),
    )(spec, raw, table)
    return (residual, gradient)


def solution(mesh):
    dims = tuple(mesh.shape[name] for name in ("freq", "rtile", "rep"))
    return jax.shard_map(
        functools.partial(shards, dims),
        mesh=mesh,
        in_specs=(
            P("rtile", "freq", None, None),
            P(None, "freq", "rep", "rtile", None, None),
            P(None, "freq", "rep", "rtile", None, None),
            P("freq", "rep", "rtile"),
            P(None, ("freq", "rtile"), "rep"),
        ),
        out_specs=(P(None, ("freq", "rtile"), "rep"), P("rtile", ("freq", "rep"), None, None)),
        check_vma=False,
    )
```

```python
import functools

import jax
import jax.numpy as jnp
import ml_dtypes
import numpy as np
from jax import lax
from jax.experimental import pallas as pl
from jax.experimental.pallas import tpu as pltpu
from jax.sharding import PartitionSpec as P

MESH = pl.DeviceIdType.MESH
BF16 = jnp.bfloat16
F32 = jnp.float32
LAST = (((1,), (1,)), ((), ()))
PLAIN = (((1,), (0,)), ((), ()))


def tables(count, length):
    bins = 1 + np.arange(count, dtype=np.int64)
    phases = (bins[:, None] * np.arange(length, dtype=np.int64)[None, :] % length).astype(
        np.float32
    ) * np.float32(2.0 * np.pi / length)
    both = np.concatenate([np.cos(phases), -np.sin(phases)], axis=0)
    return both.astype(ml_dtypes.bfloat16)


def matmul(form, first, second):
    return lax.dot_general(first, second, form, preferred_element_type=F32)


def lanes(shape):
    return lax.broadcasted_iota(jnp.int32, shape, len(shape) - 1)


def rows(shape):
    return lax.broadcasted_iota(jnp.int32, shape, len(shape) - 2)


def chain_kernel(
    dims,
    model_ref,
    left_ref,
    right_ref,
    ranks_hbm,
    data_ref,
    table_ref,
    residual_ref,
    spec_ref,
    ranks_ref,
    traces,
    table,
    left,
    right,
    stage,
    send_a,
    recv_a,
    weights,
    send_r,
    recv_sib,
    send_z,
    near_z,
    far_z,
    data,
    recv_d,
    back,
    grads,
    send_g,
    recv_g,
    load_sem,
    out_sem,
    a_sem,
    g_sem,
    sib_sem,
    near_sem,
    far_sem,
    data_sem,
    near_d_sem,
    swap_sem,
):
    n_freq, n_rtile, n_rep = dims
    n_z = n_rtile // 2
    n_slot = n_freq * n_rep
    me_f = lax.axis_index("freq")
    me_t = lax.axis_index("rtile")
    me_p = lax.axis_index("rep")
    me_slot = me_f * n_rep + me_p
    me_z = lax.div(me_t, 2)
    me_c = lax.rem(me_t, 2)
    me_k = lax.rem(me_z, 4)
    me_b = lax.div(me_z, 4)
    sibling = {"rtile": me_z * 2 + (1 - me_c)}
    group = model_ref.shape[1] // n_rep
    freq_local, row_tiles, col_tiles, rank_size, tile_size = right.shape[1:]

    def slot_device(slot):
        return {"freq": lax.div(slot, n_rep), "rep": lax.rem(slot, n_rep)}

    def hops(shift):
        return min(shift[0], 8 - shift[0]) + min(shift[1], 4 - shift[1])

    shifts = sorted(((dy, dx) for dy in range(8) for dx in range(4)), key=hops)[:0:-1]
    me_y = me_p * 4 + lax.div(me_f, 4)
    me_x = lax.rem(me_f, 4)
    peers = []
    for dy, dx in shifts:
        y = lax.rem(me_y + dy, 8)
        peers.append((lax.rem(y, 4) * 4 + lax.rem(me_x + dx, 4)) * 2 + lax.div(y, 4))

    def z_device(z):
        return {"rtile": z * 2 + me_c}

    def z_other(z):
        return {"rtile": z * 2 + (1 - me_c)}

    def slots_like(send_sem, recv_sem):
        most = recv_a.at[pl.ds(0, n_slot - 1)]
        return pltpu.make_async_remote_copy(
            src_ref=most,
            dst_ref=most,
            send_sem=send_sem,
            recv_sem=recv_sem,
            device_id=sibling,
            device_id_type=MESH,
        )

    def chunks_like(count, send_sem, recv_sem):
        most = recv_sib.at[pl.ds(0, count)]
        return pltpu.make_async_remote_copy(
            src_ref=most,
            dst_ref=most,
            send_sem=send_sem,
            recv_sem=recv_sem,
            device_id=sibling,
            device_id_type=MESH,
        )

    half_group = group // 2
    model_loads = [
        pltpu.make_async_copy(
            model_ref.at[0, pl.ds(me_p * group + part * half_group, half_group)],
            traces.at[pl.ds(part * half_group, half_group)],
            load_sem.at[6 + part],
        )
        for part in range(2)
    ]
    ranks_load = pltpu.make_async_copy(ranks_hbm, ranks_ref, load_sem.at[0])
    table_load = pltpu.make_async_copy(table_ref, table, load_sem.at[1])
    right_load = pltpu.make_async_copy(right_ref, right, load_sem.at[2])
    left_load = pltpu.make_async_copy(left_ref, left, load_sem.at[3])
    table_load.start()
    model_loads[0].start()
    model_loads[1].start()
    data_load = pltpu.make_async_copy(data_ref, data.at[me_b], load_sem.at[4])

    barrier = pltpu.get_barrier_semaphore()

    for slot in peers:
        pl.semaphore_signal(barrier, inc=1, device_id=slot_device(slot), device_id_type=MESH)
    for shift in (1, 2, n_z - 2, n_z - 1):
        pl.semaphore_signal(
            barrier, inc=1, device_id=z_other(lax.rem(me_z + shift, n_z)), device_id_type=MESH
        )
    for shift in (1, 2, 4, n_z - 4, n_z - 2, n_z - 1):
        pl.semaphore_signal(
            barrier, inc=1, device_id=z_device(lax.rem(me_z + shift, n_z)), device_id_type=MESH
        )
    pl.semaphore_signal(barrier, inc=1, device_id=sibling, device_id_type=MESH)

    data_load.start()
    right_load.start()
    left_load.start()
    ranks_load.start()

    table_load.wait()
    bins = n_freq * freq_local
    quarter = lanes((bins, 128)) // 32
    for chunk in range(group // 4):
        if chunk % 2 == 0:
            part = chunk // 2
            model_loads[part].wait()
            some = traces[part * half_group : (part + 1) * half_group]
            spectra = matmul(LAST, table[...], some.reshape(-1, traces.shape[2]))
        at = chunk % 2 * 128
        re = spectra[:bins, at : at + 128]
        im = spectra[bins:, at : at + 128]
        first = jnp.where(
            quarter == 0,
            re,
            jnp.where(
                quarter == 1,
                pltpu.roll(im, 32, 1),
                jnp.where(quarter == 2, pltpu.roll(re, 32, 1), pltpu.roll(im, 64, 1)),
            ),
        )
        second = jnp.where(
            quarter == 0,
            pltpu.roll(re, 64, 1),
            jnp.where(
                quarter == 1,
                pltpu.roll(im, 96, 1),
                jnp.where(quarter == 2, pltpu.roll(re, 96, 1), im),
            ),
        )
        stage[pl.ds(2 * chunk, bins, stride=8), :] = first
        stage[pl.ds(2 * chunk + 1, bins, stride=8), :] = second
    band = freq_local * 8
    send_a[...] = stage[...].reshape(n_freq, band, 128).astype(BF16)

    pl.semaphore_wait(barrier, n_slot - 1 + 11)

    def a_copy(target, source):
        return pltpu.make_async_remote_copy(
            src_ref=send_a.at[lax.div(target, n_rep)],
            dst_ref=recv_a.at[source],
            send_sem=out_sem.at[0],
            recv_sem=a_sem,
            device_id=slot_device(target),
            device_id_type=MESH,
        )

    for slot in peers:
        a_copy(slot, me_slot).start()

    def data_copy(shift, send_sem):
        return pltpu.make_async_remote_copy(
            src_ref=data.at[me_b],
            dst_ref=data.at[me_b],
            send_sem=send_sem,
            recv_sem=data_sem,
            device_id=z_device(lax.rem(me_z + shift, n_z)),
            device_id_type=MESH,
        )

    data_load.wait()
    data_copy(4, out_sem.at[6]).start()
    data_copy(n_z - 4, out_sem.at[6]).start()

    recv_a[me_slot] = send_a[me_f]
    right_load.wait()
    left_load.wait()
    ranks_load.wait()

    slots_like(out_sem.at[0], a_sem).wait_recv()

    per_tile = n_slot // col_tiles
    lane_p = lanes((row_tiles * rank_size, 128))
    row_k = rows((rank_size, 128))
    low4 = rows((32, tile_size)) % 8 < 4

    def sib_copy(f):
        part = pl.ds(f * 4, 4)
        return pltpu.make_async_remote_copy(
            src_ref=send_r.at[1 - me_c, part],
            dst_ref=recv_sib.at[part],
            send_sem=out_sem.at[1],
            recv_sem=sib_sem.at[f],
            device_id=sibling,
            device_id_type=MESH,
        )

    def predict(f):
        for j in range(col_tiles):
            arrived = recv_a[j * per_tile : (j + 1) * per_tile, f * 8 : (f + 1) * 8, :]
            arrived = arrived.astype(F32).reshape(per_tile * 8, 128)
            weights[pl.ds(0, per_tile * 8, stride=2), :] = arrived
            weights[pl.ds(1, per_tile * 8, stride=2), :] = pltpu.roll(arrived, 64, 1)
            columns = weights[...].astype(BF16)
            by_re = matmul(
                PLAIN, right[0, f, :, j].reshape(row_tiles * rank_size, tile_size), columns
            )
            by_im = matmul(
                PLAIN, right[1, f, :, j].reshape(row_tiles * rank_size, tile_size), columns
            )
            projected = by_re + jnp.where(
                lane_p < 32, pltpu.roll(by_im, 96, 1), -pltpu.roll(by_im, 32, 1)
            )
            for i in range(row_tiles):
                part = projected[i * rank_size : (i + 1) * rank_size]
                back[f, i, j * rank_size : (j + 1) * rank_size, :] = jnp.where(
                    row_k < ranks_ref[f, j, i], part, 0.0
                )
        for i in range(row_tiles):
            lhs = back[f, i].T[:64].astype(BF16)
            span = slice(i * tile_size, (i + 1) * tile_size)
            by_re = matmul(PLAIN, lhs, left[0, f, i].reshape(col_tiles * rank_size, tile_size))
            by_im = matmul(PLAIN, lhs, left[1, f, i].reshape(col_tiles * rank_size, tile_size))
            out_re = by_re[:32] - by_im[32:]
            out_im = by_re[32:] + by_im[:32]
            even = jnp.where(low4, out_re, pltpu.roll(out_im, 4, 0))
            odd = jnp.where(low4, pltpu.roll(out_re, 28, 0), out_im)
            send_r[0, f * 4 : (f + 1) * 4, :, span] = even.reshape(4, 8, tile_size).astype(BF16)
            send_r[1, f * 4 : (f + 1) * 4, :, span] = odd.reshape(4, 8, tile_size).astype(BF16)
        sib_copy(f).start()

    half = send_r.shape[3] // 2
    whole = pl.ds(0, 2 * half)
    first_half = pl.ds(0, half)
    second_half = pl.ds(half, half)
    near = (
        (2, 2, 2, first_half),
        (n_z - 2, 2, 2, second_half),
        (1, 1, 0, whole),
        (n_z - 1, 3, 1, whole),
    )
    def near_sends(f):
        part = pl.ds(f * 4, 4)
        sib_copy(f).wait_recv()
        send_z[part] = (send_r[me_c, part].astype(F32) + recv_sib[part].astype(F32)).astype(BF16)
        for shift, ahead, place, span in near:
            pltpu.make_async_remote_copy(
                src_ref=send_z.at[f * 4 + lax.rem(me_k + ahead, 4), :, span],
                dst_ref=near_z.at[place, f, :, span],
                send_sem=out_sem.at[2],
                recv_sem=near_sem.at[f],
                device_id=z_device(lax.rem(me_z + shift, n_z)),
                device_id_type=MESH,
            ).start()

    predict(0)
    for f in range(1, freq_local):
        predict(f)
        near_sends(f - 1)
    near_sends(freq_local - 1)

    far_shifts = (4, n_z - 4)
    for f in range(freq_local):
        chunks_like(3, out_sem.at[2], near_sem.at[f]).wait_recv()
        total = send_z[f * 4 + me_k].astype(F32)
        for place in range(3):
            total = total + near_z[place, f].astype(F32)
        far_z[me_b, f] = total.astype(BF16)
        for shift in far_shifts:
            pltpu.make_async_remote_copy(
                src_ref=far_z.at[me_b, f],
                dst_ref=far_z.at[me_b, f],
                send_sem=out_sem.at[3],
                recv_sem=far_sem.at[f],
                device_id=z_device(lax.rem(me_z + shift, n_z)),
                device_id_type=MESH,
            ).start()

    most = data.at[pl.ds(0, 2)]
    pltpu.make_async_remote_copy(
        src_ref=most,
        dst_ref=most,
        send_sem=out_sem.at[6],
        recv_sem=data_sem,
        device_id=sibling,
        device_id_type=MESH,
    ).wait()
    for f in range(freq_local):
        chunks_like(2, out_sem.at[3], far_sem.at[f]).wait_recv()
        total = far_z[0, f].astype(F32)
        for b in range(1, freq_local):
            total = total + far_z[b, f].astype(F32)
        residual_re = total[:4] - data[f, 0]
        residual_im = total[4:] - data[f, 1]
        recv_d[me_c, f * 4 + me_k] = jnp.concatenate([residual_re, residual_im], axis=0).astype(
            BF16
        )
        for shift, _, _, span in near:
            pltpu.make_async_remote_copy(
                src_ref=recv_d.at[me_c, f * 4 + me_k, :, span],
                dst_ref=recv_d.at[me_c, f * 4 + me_k, :, span],
                send_sem=out_sem.at[4],
                recv_sem=near_d_sem.at[f],
                device_id=z_device(lax.rem(me_z + shift, n_z)),
                device_id_type=MESH,
            ).start()
        if f == freq_local - 1:
            for shift, _, _, span in near:
                pltpu.make_async_remote_copy(
                    src_ref=recv_d.at[me_c, f * 4 + me_k, :, span],
                    dst_ref=recv_d.at[me_c, f * 4 + me_k, :, span],
                    send_sem=out_sem.at[7],
                    recv_sem=swap_sem.at[f],
                    device_id=z_other(lax.rem(me_z + shift, n_z)),
                    device_id_type=MESH,
                ).start()
            pltpu.make_async_remote_copy(
                src_ref=recv_d.at[me_c, f * 4 + me_k],
                dst_ref=recv_d.at[me_c, f * 4 + me_k],
                send_sem=out_sem.at[7],
                recv_sem=swap_sem.at[f],
                device_id=sibling,
                device_id_type=MESH,
            ).start()
        data[f, 0] = residual_re
        data[f, 1] = residual_im
    residual_store = pltpu.make_async_copy(data.at[me_b], residual_ref, load_sem.at[5])
    residual_store.start()

    def swap_copy(f):
        part = pl.ds(f * 4, 4)
        return pltpu.make_async_remote_copy(
            src_ref=recv_d.at[me_c, part],
            dst_ref=recv_d.at[me_c, part],
            send_sem=out_sem.at[7],
            recv_sem=swap_sem.at[f],
            device_id=sibling,
            device_id_type=MESH,
        )

    for f in range(freq_local):
        chunks_like(3, out_sem.at[4], near_d_sem.at[f]).wait_recv()
        if f < freq_local - 1:
            swap_copy(f).start()

    low4 = rows((32, recv_d.shape[3])) % 8 < 4
    row_k = rows((rank_size, 128))
    for f in range(freq_local):
        swap_copy(f).wait_recv()
        even = recv_d[0, f * 4 : (f + 1) * 4].astype(F32).reshape(32, -1)
        odd = recv_d[1, f * 4 : (f + 1) * 4].astype(F32).reshape(32, -1)
        mis_re = jnp.where(low4, even, pltpu.roll(odd, 4, 0))
        mis_im = jnp.where(low4, pltpu.roll(even, 28, 0), odd)
        top = jnp.concatenate([mis_re, mis_im, -mis_im, mis_re], axis=0).astype(BF16)
        low = jnp.concatenate([mis_im, -mis_re, mis_re, mis_im], axis=0).astype(BF16)
        for i in range(row_tiles):
            span = slice(i * tile_size, (i + 1) * tile_size)
            part = matmul(
                LAST, left[0, f, i].reshape(col_tiles * rank_size, tile_size), top[:, span]
            ) + matmul(
                LAST, left[1, f, i].reshape(col_tiles * rank_size, tile_size), low[:, span]
            )
            for j in range(col_tiles):
                grads[j, i * rank_size : (i + 1) * rank_size, :] = jnp.where(
                    row_k < ranks_ref[f, j, i], part[j * rank_size : (j + 1) * rank_size], 0.0
                )
        for j in range(col_tiles):
            lhs = grads[j].T.astype(BF16)
            spec_t = matmul(
                PLAIN, lhs[:64], right[0, f, :, j].reshape(row_tiles * rank_size, tile_size)
            ) + matmul(
                PLAIN, lhs[64:], right[1, f, :, j].reshape(row_tiles * rank_size, tile_size)
            )
            weights[:, :64] = spec_t.T
            even = weights[pl.ds(0, per_tile * 8, stride=2), :]
            odd = weights[pl.ds(1, per_tile * 8, stride=2), :]
            packed = jnp.where(lanes(even.shape) < 64, even, pltpu.roll(odd, 64, 1))
            send_g[j * per_tile : (j + 1) * per_tile, f * 8 : (f + 1) * 8, :] = packed.reshape(
                per_tile, 8, 128
            ).astype(BF16)

    def g_copy(target, source):
        return pltpu.make_async_remote_copy(
            src_ref=send_g.at[target],
            dst_ref=recv_g.at[source],
            send_sem=out_sem.at[5],
            recv_sem=g_sem,
            device_id=slot_device(target),
            device_id_type=MESH,
        )

    for slot in peers:
        g_copy(slot, me_slot).start()

    recv_g[me_slot] = send_g[me_slot]

    slots_like(out_sem.at[5], g_sem).wait_recv()

    for f in range(n_freq):
        both = recv_g[n_rep * f].astype(F32)
        for p in range(1, n_rep):
            both = both + recv_g[n_rep * f + p].astype(F32)
        stage[f * band : (f + 1) * band, :] = both
    for chunk in range(group // 4):
        first = stage[pl.ds(2 * chunk, bins, stride=8), :]
        second = stage[pl.ds(2 * chunk + 1, bins, stride=8), :]
        re = jnp.where(
            quarter == 0,
            first,
            jnp.where(
                quarter == 1,
                pltpu.roll(first, 96, 1),
                jnp.where(quarter == 2, pltpu.roll(second, 64, 1), pltpu.roll(second, 32, 1)),
            ),
        )
        im = jnp.where(
            quarter == 0,
            pltpu.roll(first, 96, 1),
            jnp.where(
                quarter == 1,
                pltpu.roll(first, 64, 1),
                jnp.where(quarter == 2, pltpu.roll(second, 32, 1), second),
            ),
        )
        spec_ref[:bins, chunk * 128 : (chunk + 1) * 128] = re.astype(BF16)
        spec_ref[bins:, chunk * 128 : (chunk + 1) * 128] = im.astype(BF16)

    slots_like(out_sem.at[0], a_sem).wait_send()
    slots_like(out_sem.at[5], g_sem).wait_send()
    for place, count in ((1, 12), (2, 9), (3, 6), (4, 9), (7, 12)):
        chunks_like(count, out_sem.at[place], g_sem).wait_send()
    residual_store.wait()


def traces_kernel(
    spec_ref, raw_ref, table_ref, residual_ref, gradient_ref, spec, table, raw, out, sems
):
    spec_load = pltpu.make_async_copy(spec_ref, spec, sems.at[0])
    table_load = pltpu.make_async_copy(table_ref, table, sems.at[1])
    raw_load = pltpu.make_async_copy(raw_ref, raw, sems.at[2])
    residual_store = pltpu.make_async_copy(raw, residual_ref, sems.at[3])
    spec_load.start()
    table_load.start()
    raw_load.start()
    _, group, rhs_count, length = gradient_ref.shape
    steps = out.shape[0]
    part = group // steps
    spec_load.wait()
    lhs = spec[...].astype(F32).T.astype(BF16)
    table_load.wait()
    raw_load.wait()
    residual_store.start()
    stores = []
    for step in range(steps):
        some = lhs[step * part * rhs_count : (step + 1) * part * rhs_count]
        out[step] = matmul(PLAIN, some, table[...]).reshape(part, rhs_count, length).astype(BF16)
        store = pltpu.make_async_copy(
            out.at[step], gradient_ref.at[0, pl.ds(step * part, part)], sems.at[4 + step]
        )
        store.start()
        stores.append(store)
    residual_store.wait()
    for store in stores:
        store.wait()


def shards(dims, model, green_left, green_right, ranks, data):
    n_freq, n_rtile, n_rep = dims
    n_z = n_rtile // 2
    n_slot = n_freq * n_rep
    _, receivers, rhs_count, length = model.shape
    group = receivers // n_rep
    freq_local = ranks.shape[0]
    row_tiles, col_tiles, rank_size, tile_size = green_left.shape[2:]
    bins = n_freq * freq_local
    sources = row_tiles * tile_size
    assert (rhs_count, tile_size, group, col_tiles) == (32, 256, 16, 2)
    assert dims == (16, 24, 2)
    assert n_z == freq_local * 4 and n_slot * group == col_tiles * tile_size
    table = jnp.asarray(tables(bins, length))
    band = freq_local * 8
    raw, spec = pl.pallas_call(
        functools.partial(chain_kernel, dims),
        out_shape=(
            jax.ShapeDtypeStruct(data.shape, F32),
            jax.ShapeDtypeStruct((2 * bins, group * rhs_count), BF16),
        ),
        in_specs=[
            pl.BlockSpec(memory_space=pltpu.HBM),
            pl.BlockSpec(memory_space=pltpu.HBM),
            pl.BlockSpec(memory_space=pltpu.HBM),
            pl.BlockSpec(memory_space=pltpu.HBM),
            pl.BlockSpec(memory_space=pltpu.HBM),
            pl.BlockSpec(memory_space=pltpu.HBM),
        ],
        out_specs=(
            pl.BlockSpec(memory_space=pltpu.HBM),
            pl.BlockSpec(memory_space=pltpu.VMEM),
        ),
        scratch_shapes=[
            pltpu.SMEM((freq_local, col_tiles, row_tiles), jnp.int32),
            pltpu.VMEM((group, rhs_count, length), BF16),
            pltpu.VMEM((2 * bins, length), BF16),
            pltpu.VMEM(green_left.shape, BF16),
            pltpu.VMEM(green_right.shape, BF16),
            pltpu.VMEM((bins * 8, 128), F32),
            pltpu.VMEM((n_freq, band, 128), BF16),
            pltpu.VMEM((n_slot, band, 128), BF16),
            pltpu.VMEM((tile_size, 128), F32),
            pltpu.VMEM((2, n_z, 8, sources), BF16),
            pltpu.VMEM((n_z, 8, sources), BF16),
            pltpu.VMEM((n_z, 8, sources), BF16),
            pltpu.VMEM((3, freq_local, 8, sources), BF16),
            pltpu.VMEM((freq_local, freq_local, 8, sources), BF16),
            pltpu.VMEM((freq_local, *data.shape), F32),
            pltpu.VMEM((2, n_z, 8, sources), BF16),
            pltpu.VMEM((freq_local, row_tiles, col_tiles * rank_size, 128), F32),
            pltpu.VMEM((col_tiles, row_tiles * rank_size, 128), F32),
            pltpu.VMEM((n_slot, band, 128), BF16),
            pltpu.VMEM((n_slot, band, 128), BF16),
            pltpu.SemaphoreType.DMA((8,)),
            pltpu.SemaphoreType.DMA((8,)),
            pltpu.SemaphoreType.DMA,
            pltpu.SemaphoreType.DMA,
            pltpu.SemaphoreType.DMA((freq_local,)),
            pltpu.SemaphoreType.DMA((freq_local,)),
            pltpu.SemaphoreType.DMA((freq_local,)),
            pltpu.SemaphoreType.DMA,
            pltpu.SemaphoreType.DMA((freq_local,)),
            pltpu.SemaphoreType.DMA((freq_local,)),
        ],
        compiler_params=pltpu.CompilerParams(
            collective_id=0, has_side_effects=True, vmem_limit_bytes=60 * 1024 * 1024
        ),
    )(model, green_left, green_right, jnp.swapaxes(ranks, 1, 2), data, table)
    steps = 4
    residual, gradient = pl.pallas_call(
        traces_kernel,
        out_shape=(
            jax.ShapeDtypeStruct(data.shape, F32),
            jax.ShapeDtypeStruct((1, group, rhs_count, length), BF16),
        ),
        in_specs=[
            pl.BlockSpec(memory_space=pltpu.HBM),
            pl.BlockSpec(memory_space=pltpu.HBM),
            pl.BlockSpec(memory_space=pltpu.HBM),
        ],
        out_specs=(
            pl.BlockSpec(memory_space=pltpu.HBM),
            pl.BlockSpec(memory_space=pltpu.HBM),
        ),
        scratch_shapes=[
            pltpu.VMEM((2 * bins, group * rhs_count), BF16),
            pltpu.VMEM((2 * bins, length), BF16),
            pltpu.VMEM(data.shape, F32),
            pltpu.VMEM((steps, group // steps, rhs_count, length), BF16),
            pltpu.SemaphoreType.DMA((4 + steps,)),
        ],
        compiler_params=pltpu.CompilerParams(vmem_limit_bytes=60 * 1024 * 1024),
    )(spec, raw, table)
    return (residual, gradient)


def solution(mesh):
    dims = tuple(mesh.shape[name] for name in ("freq", "rtile", "rep"))
    return jax.shard_map(
        functools.partial(shards, dims),
        mesh=mesh,
        in_specs=(
            P("rtile", "freq", None, None),
            P(None, "freq", "rep", "rtile", None, None),
            P(None, "freq", "rep", "rtile", None, None),
            P("freq", "rep", "rtile"),
            P(None, ("freq", "rtile"), "rep"),
        ),
        out_specs=(P(None, ("freq", "rtile"), "rep"), P("rtile", ("freq", "rep"), None, None)),
        check_vma=False,
    )
```
